256 devices in a mesh: mem: 16 (over z_hi, x), tensor: 16 (over y, z_lo, core).
Axes of the slice: x: 4, y: 4, z: 8 (z_hi: 4, z_lo: 2; z = z_hi * 2 + z_lo), core: 2. Of those that a mesh axis runs over, the one named last changes fastest.
Arguments:
- queries: bfloat16 [4096, 6144], P('mem', 'tensor'), may hold values from -180 to 180
- local_keys: bfloat16 [4096, 6144], P('mem', 'tensor'), may hold values from -6 to 6
- local_values: bfloat16 [4096, 6144], P('mem', 'tensor'), may hold values from -6 to 6
- segments: int32 [4096], P('mem'), may hold values from 0 to 15, never falling along the last dimension, each value on 1 to 512 neighbouring positions
- memory_keys: bfloat16 [8192, 6144], P('mem', 'tensor'), may hold values from -6 to 6
- memory_values: bfloat16 [8192, 6144], P('mem', 'tensor'), may hold values from -6 to 6
- retrieved: int32 [32, 8], P('mem'), may hold values from 0 to 63, as said below
- block_slot: int32 [64], replicated, may hold values from 0 to 63, as said below
- gate_bias: float32 [48], P('tensor'), may hold values from -4 to 4
- out_weight: bfloat16 [6144, 6144], P('tensor'), may hold values from -0.078125 to 0.078125
- cotangent: bfloat16 [4096, 6144], P('mem', 'tensor'), may hold values from -1.5 to 1.5
Outputs:
- attention: bfloat16 [4096, 6144], P('mem', 'tensor')
- attention_grad: bfloat16 [4096, 6144], P('mem', 'tensor')
- weight_grad: float32 [6144, 6144], P('tensor', 'mem')
The draws below stay inside these ranges and needn't reach their ends.
Inputs may be any that keep to these rules, and one draw needn't show every extreme that they name: `retrieved`: within a row the 8 ids are distinct and stored in distinct memory shards (shard of id b: block_slot[b] // 4). The 2 consecutive rows of one data group name at most 2 distinct ids stored in any one shard; in every draw every data group names at least one shard twice. `block_slot`: each value once; memory block b is row block block_slot[b] of memory_keys and memory_values. `segments`: segment ids never fall along the rows; a segment has 1 to 512 rows.
All inputs are finite; a program needn't handle non-finite values.
Results may differ from the reference program's by a relative error of at most 0.015.
Values may be sent and summed in bfloat16 or wider, within the bound.
No kernel may reach another device: no remote copies, remote signals or barrier semaphores. Data moves between devices by JAX's collectives and lax.ppermute only.
A program may use at most 64 MiB of HBM per device.

```python
import math
import jax
import jax.numpy as jnp
import numpy as np
from jax import lax

D = 6144
H = 48
HEAD = 128
BLOCK = 128
TOPK = 8
CAP = 2
TOK_DEV = 256
MEMBLK_DEV = 4
QB_DEV = 2
TOKENS = 4096
QBLOCKS = 32
NBLOCKS = 64
MEMROWS = 8192
HD = 6144


def shared_order(key):
    return jax.random.permutation(jax.random.fold_in(key, 7), NBLOCKS)


def draw_block_slot(key, part):
    return shared_order(key).astype(jnp.int32)


def draw_retrieved(key, part):
    group_count = NBLOCKS // MEMBLK_DEV
    inverse = jnp.argsort(shared_order(key)).astype(jnp.int32)
    key_hot, key_start, key_pick, key_rotate = jax.random.split(jax.random.fold_in(key, 11), 4)
    hottest = jax.random.randint(key_hot, (), 0, group_count)
    row_starts = jax.random.randint(key_start, (QBLOCKS,), 0, group_count)
    row_place = jnp.arange(QBLOCKS, dtype=jnp.int32) % QB_DEV
    row_starts = jnp.where(row_place < CAP, hottest, row_starts)
    owners = (row_starts[:, None] + jnp.arange(TOPK, dtype=jnp.int32)[None, :]) % group_count
    pick_ids = jax.random.randint(key_pick, (QBLOCKS, TOPK), 0, CAP)
    pick_ids = pick_ids.at[:, 0].set(jnp.where(row_place < CAP, row_place, pick_ids[:, 0]))
    rotation = jax.random.randint(key_rotate, (group_count, group_count), 0, MEMBLK_DEV)
    requester = jnp.arange(QBLOCKS, dtype=jnp.int32) // QB_DEV
    local_slot = (rotation[requester[:, None], owners] + pick_ids) % MEMBLK_DEV
    return inverse[owners * MEMBLK_DEV + local_slot].astype(jnp.int32)


def draw_queries(key, part):
    key_base = jax.random.fold_in(jax.random.fold_in(key, 3), 0)
    values = jnp.clip(jax.random.normal(key_base, (TOKENS, HD), jnp.float32) * 2.0, -8.0, 8.0)
    return values.astype(jnp.bfloat16)


def with_spikes(array, rng, source, target, blocks, factor):
    def block_of(position):
        return (jnp.arange(array.shape[position]) // (array.shape[position] // blocks)).reshape((-1,) + (1,) * (array.ndim - 1 - position))

    first = jax.random.permutation(rng, blocks)[block_of(target)]
    second = (block_of(target) + blocks // 2) % blocks
    return jnp.where((block_of(source) == first) | (block_of(source) == second), factor * array, array)


def steps_of(own_key, dims, pieces, least, largest):
    gain, own = 1.0, jax.random.fold_in(own_key, 6)
    for dim, parts in pieces:
        steps = jnp.exp(jax.random.uniform(jax.random.fold_in(own, dim), (parts,), jnp.float32, least / len(pieces), largest / len(pieces)))
        gain = gain * jnp.repeat(steps, dims[dim] // parts).reshape([-1 if axis == dim else 1 for axis in range(len(dims))])
    return gain


def profile(number_of, total, bound, slope):
    weights = [(1 << 20) // math.isqrt(standing ** slope) + 1 for standing in range(2, number_of + 1)]
    rest, given = total - bound - (number_of - 1), [1] * (number_of - 1)
    while rest > 0:
        free = [i for i in range(number_of - 1) if given[i] < bound]
        whole, budget = sum([weights[i] for i in free]), rest
        for i in free:
            addition = min(bound - given[i], max(1, budget * weights[i] // whole), rest)
            given[i] = given[i] + addition
            rest = rest - addition
    return np.array([bound] + given)


def uneven(rng, amount, total, most, skew):
    if amount == 2:
        one = jax.random.randint(rng, (), max(1, total - most), min(most, total - 1) + 1)
        return jnp.stack([one, total - one])
    tallies = jnp.asarray(profile(amount, total, most, skew), jnp.int32)
    couples = (amount - 1) // 2
    donor, taker = tallies[1:1 + 2 * couples:2], tallies[2:2 + 2 * couples:2]
    room = jnp.minimum(donor - 1, most - taker)
    passed = jax.random.randint(jax.random.fold_in(rng, 1), (couples,), 0, 1 << 20) % (room + 1)
    tallies = tallies.at[1:1 + 2 * couples:2].set(donor - passed).at[2:2 + 2 * couples:2].set(taker + passed)
    return tallies[jax.random.permutation(jax.random.fold_in(rng, 2), amount)]


def centred(own_key, dims, deviation, bound, cuts=(), kind=jnp.bfloat16):
    values = deviation * jax.random.normal(own_key, dims, jnp.float32)
    if cuts:
        values = values * steps_of(own_key, dims, cuts, -0.22, 0.18)
    return jnp.clip(values, -bound, bound).astype(kind)


def bell_draw_with(stream_key, dims, scale, bound, shards, heavy, kind=jnp.bfloat16):
    values = scale * jax.random.normal(stream_key, dims, jnp.float32)
    if shards:
        values = values * steps_of(stream_key, dims, shards, -0.22, 0.18)
    return jnp.clip(with_spikes(values, jax.random.fold_in(stream_key, 3), *heavy), -bound, bound).astype(kind)


def setup_inputs(seed: int = 0) -> dict:
    streams_of = jax.random.split(jax.random.key(seed), 12)
    return {
        "queries": draw_queries(jax.random.fold_in(streams_of[11], 71), 0),
        "local_keys": centred(streams_of[1], (TOKENS, HD), 1.0, 6.0, ((0, 16), (1, 16))),
        "local_values": centred(streams_of[2], (TOKENS, HD), 1.0, 6.0, ((0, 16), (1, 16))),
        "segments": jnp.searchsorted(jnp.cumsum(uneven(streams_of[3], TOKENS // (2 * BLOCK), TOKENS, 4 * BLOCK, 2)), jnp.arange(TOKENS), side="right").astype(jnp.int32),
        "memory_keys": centred(streams_of[4], (MEMROWS, HD), 1.0, 6.0, ((0, 16), (1, 16))),
        "memory_values": centred(streams_of[5], (MEMROWS, HD), 1.0, 6.0, ((0, 16), (1, 16))),
        "retrieved": draw_retrieved(jax.random.fold_in(streams_of[11], 71), 0),
        "block_slot": draw_block_slot(jax.random.fold_in(streams_of[11], 71), 0),
        "gate_bias": centred(streams_of[8], (H,), 1.5, 4.0, ((0, 16),), jnp.float32),
        "out_weight": centred(streams_of[9], (HD, D), HD ** -0.5, 0.078125, ((0, 16),)),
        "cotangent": bell_draw_with(streams_of[10], (TOKENS, D), 0.25, 1.5, ((0, 16), (1, 16)), (0, 1, 16, 2.0)),
    }


masked_score = -1e30


def rounded_probs(scores):
    row_max = jnp.max(scores, axis=-1, keepdims=True)
    weights = jnp.exp(scores - row_max)
    totals = jnp.sum(weights, axis=-1, keepdims=True)
    return (weights / totals).astype(jnp.bfloat16)


def reference(queries, local_keys, local_values, segments, memory_keys, memory_values, retrieved, block_slot, gate_bias, out_weight, cotangent):
    scale = HEAD ** -0.5
    group_total = TOKENS // TOK_DEV
    positions = jnp.arange(TOK_DEV, dtype=jnp.int32)

    def local_group(number):
        offset = (number * TOK_DEV).astype(jnp.int32)
        query_rows = lax.dynamic_slice_in_dim(queries, offset, TOK_DEV, 0).astype(jnp.float32).reshape(TOK_DEV, H, HEAD)
        key_rows = lax.dynamic_slice_in_dim(local_keys, offset, TOK_DEV, 0).astype(jnp.float32).reshape(TOK_DEV, H, HEAD)
        value_rows = lax.dynamic_slice_in_dim(local_values, offset, TOK_DEV, 0).astype(jnp.float32).reshape(TOK_DEV, H, HEAD)
        group_segments = lax.dynamic_slice_in_dim(segments, offset, TOK_DEV, 0)
        allowed = (positions[None, :] <= positions[:, None]) & (group_segments[None, :] == group_segments[:, None])
        scores = jnp.einsum("qhd,khd->hqk", query_rows, key_rows) * scale
        scores = jnp.where(allowed[None, :, :], scores, masked_score)
        weights = lax.optimization_barrier(rounded_probs(scores)).astype(jnp.float32)
        return jnp.einsum("hqk,khd->qhd", weights, value_rows)

    local_out = lax.map(local_group, jnp.arange(group_total, dtype=jnp.int32)).reshape(TOKENS, H, HEAD)

    storage = block_slot[retrieved]
    stored_keys = memory_keys.reshape(NBLOCKS, BLOCK, H, HEAD)
    stored_values = memory_values.reshape(NBLOCKS, BLOCK, H, HEAD)

    def memory_block(number):
        offset = (number * BLOCK).astype(jnp.int32)
        query_rows = lax.dynamic_slice_in_dim(queries, offset, BLOCK, 0).astype(jnp.float32).reshape(BLOCK, H, HEAD)
        picked = storage[number]
        key_rows = stored_keys[picked].reshape(TOPK * BLOCK, H, HEAD).astype(jnp.float32)
        value_rows = stored_values[picked].reshape(TOPK * BLOCK, H, HEAD).astype(jnp.float32)
        scores = jnp.einsum("qhd,khd->hqk", query_rows, key_rows) * scale
        weights = lax.optimization_barrier(rounded_probs(scores)).astype(jnp.float32)
        return jnp.einsum("hqk,khd->qhd", weights, value_rows)

    memory_out = lax.map(memory_block, jnp.arange(QBLOCKS, dtype=jnp.int32)).reshape(TOKENS, H, HEAD)

    gate_weight = jax.nn.sigmoid(gate_bias)[None, :, None]
    attention = (gate_weight * memory_out + (1.0 - gate_weight) * local_out).reshape(TOKENS, HD).astype(jnp.bfloat16)

    attention_grad = jnp.dot(cotangent, out_weight.T, preferred_element_type=jnp.float32).astype(jnp.bfloat16)

    def add_group(running, number):
        offset = (number * TOK_DEV).astype(jnp.int32)
        attention_rows = lax.dynamic_slice_in_dim(attention, offset, TOK_DEV, 0)
        cotangent_rows = lax.dynamic_slice_in_dim(cotangent, offset, TOK_DEV, 0)
        partial_value = jnp.dot(attention_rows.T, cotangent_rows, preferred_element_type=jnp.float32).astype(jnp.bfloat16)
        partial_value = lax.optimization_barrier(partial_value).astype(jnp.float32)
        return running + partial_value, None

    weight_grad, _ = lax.scan(add_group, jnp.zeros((HD, D), jnp.float32), jnp.arange(group_total, dtype=jnp.int32))
    return (attention, attention_grad, weight_grad)
```

```python
import jax
import jax.numpy as jnp
from jax import lax
from jax.experimental import pallas as pl
from jax.experimental.pallas import tpu as pltpu
from jax.sharding import PartitionSpec as P

HEAD = 128
BLOCK = 128
SLOTS = 4
NX = 4
NZ = 4
NY = 4
LOG2E = 1.4426950408889634
SCALE2 = HEAD**-0.5 * LOG2E
NEG = -1e30
EXTRA = 16

VM = pl.BlockSpec(memory_space=pltpu.VMEM)
SM = pl.BlockSpec(memory_space=pltpu.SMEM)


def dot_nt(a, b):
    return lax.dot_general(a, b, (((1,), (1,)), ((), ())), preferred_element_type=jnp.float32)


def dot_nn(a, b):
    return lax.dot_general(a, b, (((1,), (0,)), ((), ())), preferred_element_type=jnp.float32)


def shift_x(value, k):
    pairs = [(z * NX + x, z * NX + (x + k) % NX) for z in range(NZ) for x in range(NX)]
    return lax.ppermute(value, "mem", pairs)


def shift_z(value, k):
    pairs = [(z * NX + x, (z + k) % NZ * NX + x) for z in range(NZ) for x in range(NX)]
    return lax.ppermute(value, "mem", pairs)


def shift_y(value, k):
    pairs = [(y * 4 + r, (y + k) % NY * 4 + r) for y in range(NY) for r in range(4)]
    return lax.ppermute(value, "tensor", pairs)


def flip_tensor(value, bit):
    return lax.ppermute(value, "tensor", [(t, t ^ bit) for t in range(16)])


def swap_zy(value):
    pairs = []
    for z in range(NZ):
        for x in range(NX):
            for y in range(NY):
                for r in range(4):
                    pairs.append(((z * NX + x) * 16 + y * 4 + r, (y * NX + x) * 16 + z * 4 + r))
    return lax.ppermute(value, ("mem", "tensor"), pairs)


def local_kernel(gate_ref, seg_ref, q_ref, k_ref, v_ref, out_ref):
    rows = q_ref.shape[0]
    heads = q_ref.shape[1] // HEAD
    seg_cols = jnp.broadcast_to(seg_ref[...].astype(jnp.float32), (rows, rows))
    seg_rows = seg_cols.T
    row_ids = lax.broadcasted_iota(jnp.int32, (rows, rows), 0)
    col_ids = lax.broadcasted_iota(jnp.int32, (rows, rows), 1)
    allowed = (col_ids <= row_ids) & (seg_cols == seg_rows)
    for h in range(heads):
        cols = pl.ds(h * HEAD, HEAD)
        scores = jnp.where(allowed, dot_nt(q_ref[:, cols], k_ref[:, cols]) * SCALE2, NEG)
        top = jnp.max(scores, axis=1, keepdims=True)
        weights = jnp.exp2(scores - top)
        total = jnp.sum(weights, axis=1, keepdims=True)
        out = dot_nn(weights.astype(jnp.bfloat16), v_ref[:, cols])
        out_ref[:, cols] = out * ((1.0 - gate_ref[h]) / total)


def memory_kernel(sel_ref, *refs):
    q_refs, k_refs, v_refs, out_refs = refs[0:4], refs[4:8], refs[8:12], refs[12:16]
    heads = k_refs[0].shape[1] // HEAD
    lane = lax.broadcasted_iota(jnp.int32, (BLOCK, BLOCK), 1)
    for j in range(NZ):
        q_ref, out_ref = q_refs[j], out_refs[j]

        for b in range(2):
            row = b * BLOCK
            stat = jnp.zeros((BLOCK, BLOCK), jnp.float32)
            starts, biases = [], []
            for i in range(NX):
                slot = sel_ref[(2 * j + b) * NX + i]
                starts.append(pl.multiple_of(jnp.maximum(slot, 0) * BLOCK, BLOCK))
                biases.append(jnp.where(slot >= 0, 0.0, NEG))
            for h in range(heads):
                cols = pl.ds(h * HEAD, HEAD)
                query = q_ref[pl.ds(row, BLOCK), cols]
                scores = [
                    dot_nt(query, k_refs[i][pl.ds(starts[i], BLOCK), cols]) * SCALE2 + biases[i]
                    for i in range(NX)
                ]
                peak = jnp.maximum(
                    jnp.maximum(scores[0], scores[1]), jnp.maximum(scores[2], scores[3])
                )
                top = jnp.max(peak, axis=1, keepdims=True)
                weights = [jnp.exp2(s - top) for s in scores]
                total = jnp.sum(
                    (weights[0] + weights[1]) + (weights[2] + weights[3]), axis=1, keepdims=True
                )
                acc = None
                for i in range(NX):
                    part = dot_nn(
                        weights[i].astype(jnp.bfloat16), v_refs[i][pl.ds(starts[i], BLOCK), cols]
                    )
                    acc = part if acc is None else acc + part
                out_ref[pl.ds(row, BLOCK), cols] = (acc / total).astype(jnp.bfloat16)
                stat = jnp.where(lane == h, top + jnp.log2(total), stat)
            stat = stat.T[0:8]
            high = stat.astype(jnp.bfloat16)
            rest = stat - high.astype(jnp.float32)
            mid = rest.astype(jnp.bfloat16)
            low = rest - mid.astype(jnp.float32)
            packed = jnp.concatenate(
                [
                    high[0:4].astype(jnp.float32),
                    mid[0:4].astype(jnp.float32),
                    low[0:4],
                    jnp.zeros((4, BLOCK), jnp.float32),
                ],
                axis=0,
            )
            out_ref[2 * BLOCK : 2 * BLOCK + EXTRA, pl.ds(row, BLOCK)] = packed.astype(jnp.bfloat16)
        out_ref[2 * BLOCK : 2 * BLOCK + EXTRA, 2 * BLOCK :] = jnp.zeros(
            (EXTRA, out_ref.shape[1] - 2 * BLOCK), jnp.bfloat16
        )


def merge_kernel(gate_ref, local_ref, p0, p1, p2, p3, att_ref, att_t_ref):
    parts = (p0, p1, p2, p3)
    heads = local_ref.shape[1] // HEAD
    for b in range(2):
        rows = pl.ds(b * BLOCK, BLOCK)
        logs = []
        for p in parts:
            s = p[2 * BLOCK : 2 * BLOCK + EXTRA, rows].astype(jnp.float32)
            logs.append((s[0:4] + s[4:8]) + s[8:12])
        top = jnp.maximum(jnp.maximum(logs[0], logs[1]), jnp.maximum(logs[2], logs[3]))
        shares = [jnp.exp2(s - top) for s in logs]
        total = (shares[0] + shares[1]) + (shares[2] + shares[3])
        shares = [s / total for s in shares]
        table = jnp.concatenate(shares + [jnp.zeros((BLOCK - 16, BLOCK), jnp.float32)], axis=0).T
        for h in range(heads):
            cols = pl.ds(h * HEAD, HEAD)
            acc = None
            for n, p in enumerate(parts):
                term = p[rows, cols].astype(jnp.float32) * table[:, 4 * n + h : 4 * n + h + 1]
                acc = term if acc is None else acc + term
            out = gate_ref[h] * acc + local_ref[rows, cols]
            att_ref[rows, cols] = out.astype(jnp.bfloat16)
            att_t_ref[cols, rows] = out.T.astype(jnp.bfloat16)


def grad_kernel(ids_ref, *refs):
    own, other, w_ref, out_ref, acc_ref = refs[0:4], refs[4:8], refs[8], refs[9], refs[10]
    step = pl.program_id(0)
    zl, c = ids_ref[4], ids_ref[5]
    width = own[0].shape[1]
    rows = out_ref.shape[0]

    @pl.when(step == 0)
    def _():
        acc_ref[...] = jnp.zeros_like(acc_ref)

    for k in range(NY):

        @pl.when(step == k)
        def _(k=k):
            acc = acc_ref[...]
            for w, arrays in enumerate((own, other)):
                for s in range(2):
                    place = (zl ^ s) * 2 + (c ^ w)
                    cols = pl.ds(pl.multiple_of(place * width, 128), width)
                    acc = acc + dot_nt(arrays[k][s * rows : (s + 1) * rows, :], w_ref[:, cols])
            acc_ref[...] = acc

    @pl.when(step == NY - 1)
    def _():
        out_ref[...] = acc_ref[...].astype(jnp.bfloat16)


def weight_kernel(ids_ref, *refs):
    atts, own, other = refs[0:4], refs[4:8], refs[8:12]
    outs, att_scr = refs[12:16], refs[16]
    z, x, y, zl, c = ids_ref[0], ids_ref[1], ids_ref[2], ids_ref[4], ids_ref[5]
    rows = att_scr.shape[2]
    for j in range(NZ):
        att_scr[(z - j) & 3] = atts[j][...]
    for w, arrays in enumerate((own, other)):
        for s in range(2):
            acc = None
            for k in range(NY):
                block = arrays[k][(2 + s) * rows : (3 + s) * rows, :]
                part = dot_nn(att_scr[(y - k) & 3], block)
                acc = part if acc is None else acc + part
            target = (((zl ^ s) * 2 + (c ^ w)) - x) & 3

            for n in range(NX):

                @pl.when(target == n)
                def _(n=n, acc=acc):
                    outs[n][...] = acc.astype(outs[n].dtype)


def per_device(
    queries,
    local_keys,
    local_values,
    segments,
    memory_keys,
    memory_values,
    retrieved,
    block_slot,
    gate_bias,
    out_weight,
    cotangent,
):
    rows, width = queries.shape
    heads = width // HEAD
    mem, ten = lax.axis_index("mem"), lax.axis_index("tensor")
    z, x = mem // NX, mem % NX
    y, zl, c = ten // 4, (ten // 2) % 2, ten % 2
    ids = jnp.stack([z, x, y, jnp.zeros_like(z), zl, c]).astype(jnp.int32)
    gate = jax.nn.sigmoid(gate_bias)
    params = pltpu.CompilerParams(vmem_limit_bytes=48 << 20)

    names = jnp.arange(block_slot.shape[0], dtype=jnp.int32)
    storage = jnp.sum(
        jnp.where(retrieved.reshape(-1)[:, None] == names[None, :], block_slot[None, :], 0), axis=1
    )
    extra = jnp.zeros((EXTRA, width), jnp.bfloat16)
    extra = extra.at[0, 0 : storage.shape[0]].set(storage.astype(jnp.bfloat16))
    q_pack = jnp.concatenate([queries, extra], axis=0)

    k1, v3 = shift_x(memory_keys, 1), shift_x(memory_values, -1)
    k3, v1 = shift_x(memory_keys, -1), shift_x(memory_values, 1)
    k2, v2 = shift_x(k1, 1), shift_x(v3, -1)
    q_all = [q_pack] + [shift_z(q_pack, j) for j in (1, 2, 3)]

    stored = jnp.stack([q[rows, 0:16].astype(jnp.int32) for q in q_all]).reshape(8, 8)
    shards = z * NX + (x - jnp.arange(NX, dtype=jnp.int32)) % NX
    hit = (stored // SLOTS)[:, None, :] == shards[None, :, None]
    sel = (jnp.sum(jnp.where(hit, (stored % SLOTS)[:, None, :] + 1, 0), axis=2) - 1).reshape(-1)

    both = jnp.concatenate([cotangent, swap_zy(cotangent)], axis=0)
    pair = flip_tensor(both, 2)
    quad = jnp.concatenate([both[:rows], pair[:rows], both[rows:], pair[rows:]], axis=0)
    own = [quad] + [shift_y(quad, k) for k in (1, 2, 3)]
    other = [flip_tensor(a, 1) for a in own]

    local_out = pl.pallas_call(
        local_kernel,
        out_shape=jax.ShapeDtypeStruct((rows, width), jnp.float32),
        in_specs=[SM] + [VM] * 4,
        out_specs=VM,
        compiler_params=params,
        name="local_attention",
    )(gate, segments.reshape(1, rows), queries, local_keys, local_values)

    parts = pl.pallas_call(
        memory_kernel,
        out_shape=[jax.ShapeDtypeStruct((rows + EXTRA, width), jnp.bfloat16)] * 4,
        in_specs=[SM] + [VM] * 12,
        out_specs=[VM] * 4,
        compiler_params=params,
        name="memory_attention",
    )(sel, *q_all, memory_keys, k1, k2, k3, memory_values, v1, v2, v3)

    back = [parts[0]] + [shift_z(parts[j], -j) for j in (1, 2, 3)]
    attention, att_t = pl.pallas_call(
        merge_kernel,
        out_shape=[
            jax.ShapeDtypeStruct((rows, width), jnp.bfloat16),
            jax.ShapeDtypeStruct((width, rows), jnp.bfloat16),
        ],
        in_specs=[SM] + [VM] * 5,
        out_specs=[VM] * 2,
        compiler_params=params,
        name="merge",
    )(gate, local_out, *back)

    attention_grad = pl.pallas_call(
        grad_kernel,
        out_shape=jax.ShapeDtypeStruct((rows, width), jnp.bfloat16),
        grid_spec=pltpu.PrefetchScalarGridSpec(
            num_scalar_prefetch=1,
            grid=(NY,),
            in_specs=[pl.BlockSpec((4 * rows, width), lambda g, ids: (0, 0))] * 8
            + [pl.BlockSpec((width, 4 * width), lambda g, ids: (0, (ids[2] - g) & 3))],
            out_specs=pl.BlockSpec((rows, width), lambda g, ids: (0, 0)),
            scratch_shapes=[pltpu.VMEM((rows, width), jnp.float32)],
        ),
        compiler_params=params,
        name="attention_grad",
    )(ids, *own, *other, out_weight)

    att_all = [att_t] + [shift_z(att_t, j) for j in (1, 2, 3)]
    mine, *sent = pl.pallas_call(
        weight_kernel,
        out_shape=[jax.ShapeDtypeStruct((width, width), jnp.float32)]
        + [jax.ShapeDtypeStruct((width, width), jnp.bfloat16)] * 3,
        in_specs=[SM] + [VM] * 12,
        out_specs=[VM] * 4,
        scratch_shapes=[pltpu.VMEM((NZ, width, rows), jnp.bfloat16)],
        compiler_params=params,
        name="weight_partials",
    )(ids, *att_all, *own, *other)
    got = [shift_x(sent[n - 1], n) for n in (1, 2, 3)]
    weight_grad = (mine + got[0].astype(jnp.float32)) + (
        got[1].astype(jnp.float32) + got[2].astype(jnp.float32)
    )
    return (attention, attention_grad, weight_grad)


def solution(mesh):
    return jax.shard_map(
        per_device,
        mesh=mesh,
        in_specs=(
            P("mem", "tensor"),
            P("mem", "tensor"),
            P("mem", "tensor"),
            P("mem"),
            P("mem", "tensor"),
            P("mem", "tensor"),
            P("mem", None),
            P(),
            P("tensor"),
            P("tensor", None),
            P("mem", "tensor"),
        ),
        out_specs=(P("mem", "tensor"), P("mem", "tensor"), P("tensor", "mem")),
        check_vma=False,
    )
```

```python
import jax
import jax.numpy as jnp
from jax import lax
from jax.experimental import pallas as pl
from jax.experimental.pallas import tpu as pltpu
from jax.sharding import PartitionSpec as P

HEAD = 128
BLOCK = 128
SLOTS = 4
NX = 4
NZ = 4
NY = 4
LOG2E = 1.4426950408889634
SCALE2 = HEAD**-0.5 * LOG2E
NEG = -1e30
EXTRA = 16

VM = pl.BlockSpec(memory_space=pltpu.VMEM)
SM = pl.BlockSpec(memory_space=pltpu.SMEM)
HB = pl.BlockSpec(memory_space=pltpu.HBM)


def in_hbm(values):
    return [pltpu.with_memory_space_constraint(v, pltpu.HBM) for v in values]


def together(*values):
    return lax.optimization_barrier(values)


def after(value, *deps):
    return lax.optimization_barrier((value, *deps))[0]


def dot_nt(a, b):
    return lax.dot_general(a, b, (((1,), (1,)), ((), ())), preferred_element_type=jnp.float32)


def dot_nn(a, b):
    return lax.dot_general(a, b, (((1,), (0,)), ((), ())), preferred_element_type=jnp.float32)


def shift_x(value, k):
    pairs = [(z * NX + x, z * NX + (x + k) % NX) for z in range(NZ) for x in range(NX)]
    return lax.ppermute(value, "mem", pairs)


def exchange_z(value):
    groups = [[z * NX + x for z in range(NZ)] for x in range(NX)]
    return lax.all_to_all(
        value, "mem", split_axis=0, concat_axis=0, axis_index_groups=groups, tiled=True
    )


def shift_y(value, k):
    pairs = [(y * 4 + r, (y + k) % NY * 4 + r) for y in range(NY) for r in range(4)]
    return lax.ppermute(value, "tensor", pairs)


def flip_tensor(value, bit):
    return lax.ppermute(value, "tensor", [(t, t ^ bit) for t in range(16)])


def swap_zy(value):
    pairs = []
    for z in range(NZ):
        for x in range(NX):
            for y in range(NY):
                for r in range(4):
                    pairs.append(((z * NX + x) * 16 + y * 4 + r, (y * NX + x) * 16 + z * 4 + r))
    return lax.ppermute(value, ("mem", "tensor"), pairs)


def local_kernel(gate_ref, seg_ref, q_ref, k_ref, v_ref, out_ref):
    rows = q_ref.shape[0]
    heads = q_ref.shape[1] // HEAD
    seg_cols = jnp.broadcast_to(seg_ref[...].astype(jnp.float32), (rows, rows))
    seg_rows = seg_cols.T
    row_ids = lax.broadcasted_iota(jnp.int32, (rows, rows), 0)
    col_ids = lax.broadcasted_iota(jnp.int32, (rows, rows), 1)
    allowed = (col_ids <= row_ids) & (seg_cols == seg_rows)
    for h in range(heads):
        cols = pl.ds(h * HEAD, HEAD)
        scores = jnp.where(allowed, dot_nt(q_ref[:, cols], k_ref[:, cols]) * SCALE2, NEG)
        top = jnp.max(scores, axis=1, keepdims=True)
        weights = jnp.exp2(scores - top)
        total = jnp.sum(weights, axis=1, keepdims=True)
        out = dot_nn(weights.astype(jnp.bfloat16), v_ref[:, cols])
        out_ref[:, cols] = out * ((1.0 - gate_ref[h]) / total)


def memory_kernel(sel_ref, *refs):
    sources, result_ref = refs[0:9], refs[9]
    q_buf, k_buf, v_buf, sems = refs[10:14]
    targets = [q_buf] + [buf.at[n] for buf in (k_buf, v_buf) for n in range(4)]
    copies = [
        pltpu.make_async_copy(src, dst, sems.at[n])
        for n, (src, dst) in enumerate(zip(sources, targets))
    ]
    for copy in copies:
        copy.start()
    for copy in copies:
        copy.wait()
    q_refs, k_refs, v_refs = [[buf.at[n] for n in range(4)] for buf in (q_buf, k_buf, v_buf)]
    heads = k_buf.shape[2] // HEAD
    lane = lax.broadcasted_iota(jnp.int32, (BLOCK, BLOCK), 1)
    for j in range(NZ):
        q_ref, out_ref = q_refs[j], result_ref.at[j]

        for b in range(2):
            row = b * BLOCK
            stat = jnp.zeros((BLOCK, BLOCK), jnp.float32)
            starts, biases = [], []
            for i in range(NX):
                slot = sel_ref[(2 * j + b) * NX + i]
                starts.append(pl.multiple_of(jnp.maximum(slot, 0) * BLOCK, BLOCK))
                biases.append(
                    jnp.full((1, BLOCK), jnp.where(slot >= 0, 0.0, NEG), jnp.float32)
                )
            bias = jnp.concatenate(biases, axis=1)
            for h in range(heads):
                cols = pl.ds(h * HEAD, HEAD)
                query = q_ref[pl.ds(row, BLOCK), cols]
                keys = jnp.concatenate([k_refs[i][pl.ds(starts[i], BLOCK), cols] for i in range(NX)])
                values = jnp.concatenate(
                    [v_refs[i][pl.ds(starts[i], BLOCK), cols] for i in range(NX)]
                )
                scores = dot_nt(query, keys) * SCALE2 + bias
                top = jnp.max(scores, axis=1, keepdims=True)
                weights = jnp.exp2(scores - top)
                total = jnp.sum(weights, axis=1, keepdims=True)
                acc = dot_nn(weights.astype(jnp.bfloat16), values)
                out_ref[pl.ds(row, BLOCK), cols] = (acc / total).astype(jnp.bfloat16)
                stat = jnp.where(lane == h, top + jnp.log2(total), stat)
            stat = stat.T[0:8]
            high = stat.astype(jnp.bfloat16)
            rest = stat - high.astype(jnp.float32)
            mid = rest.astype(jnp.bfloat16)
            low = rest - mid.astype(jnp.float32)
            packed = jnp.concatenate(
                [
                    high[0:4].astype(jnp.float32),
                    mid[0:4].astype(jnp.float32),
                    low[0:4],
                    jnp.zeros((4, BLOCK), jnp.float32),
                ],
                axis=0,
            )
            out_ref[2 * BLOCK : 2 * BLOCK + EXTRA, pl.ds(row, BLOCK)] = packed.astype(jnp.bfloat16)
        out_ref[2 * BLOCK : 2 * BLOCK + EXTRA, 2 * BLOCK :] = jnp.zeros(
            (EXTRA, out_ref.shape[1] - 2 * BLOCK), jnp.bfloat16
        )


def merge_kernel(gate_ref, local_ref, back_ref, att_ref, att_t_ref):
    parts = [back_ref.at[n] for n in range(NZ)]
    heads = local_ref.shape[1] // HEAD
    for b in range(2):
        rows = pl.ds(b * BLOCK, BLOCK)
        logs = []
        for p in parts:
            s = p[2 * BLOCK : 2 * BLOCK + EXTRA, rows].astype(jnp.float32)
            logs.append((s[0:4] + s[4:8]) + s[8:12])
        top = jnp.maximum(jnp.maximum(logs[0], logs[1]), jnp.maximum(logs[2], logs[3]))
        shares = [jnp.exp2(s - top) for s in logs]
        total = (shares[0] + shares[1]) + (shares[2] + shares[3])
        shares = [s / total for s in shares]
        table = jnp.concatenate(shares + [jnp.zeros((BLOCK - 16, BLOCK), jnp.float32)], axis=0).T
        for h in range(heads):
            cols = pl.ds(h * HEAD, HEAD)
            acc = None
            for n, p in enumerate(parts):
                term = p[rows, cols].astype(jnp.float32) * table[:, 4 * n + h : 4 * n + h + 1]
                acc = term if acc is None else acc + term
            out = gate_ref[h] * acc + local_ref[rows, cols]
            att_ref[rows, cols] = out.astype(jnp.bfloat16)
            flipped = out.T.astype(jnp.bfloat16)
            for n in range(NZ):
                att_t_ref[n, cols, rows] = flipped


def grad_kernel(ids_ref, *refs):
    own, other, w_ref, out_ref, acc_ref = refs[0:4], refs[4:8], refs[8], refs[9], refs[10]
    step = pl.program_id(0)
    zl, c = ids_ref[4], ids_ref[5]
    width = own[0].shape[1]
    rows = out_ref.shape[0]

    @pl.when(step == 0)
    def _():
        acc_ref[...] = jnp.zeros_like(acc_ref)

    for k in range(NY):

        @pl.when(step == k)
        def _(k=k):
            acc = acc_ref[...]
            for w, arrays in enumerate((own, other)):
                for s in range(2):
                    place = (zl ^ s) * 2 + (c ^ w)
                    cols = pl.ds(pl.multiple_of(place * width, 128), width)
                    acc = acc + dot_nt(arrays[k][s * rows : (s + 1) * rows, :], w_ref[:, cols])
            acc_ref[...] = acc

    @pl.when(step == NY - 1)
    def _():
        out_ref[...] = acc_ref[...].astype(jnp.bfloat16)


def weight_kernel(ids_ref, *refs):
    att_ref, own, other = refs[0], refs[1:5], refs[5:9]
    outs, att_scr, cot_buf, sems = refs[9:13], refs[13], refs[14], refs[15]
    x, y, zl, c = ids_ref[1], ids_ref[2], ids_ref[4], ids_ref[5]
    rows = att_ref.shape[2]
    copies = []
    for w, arrays in enumerate((own, other)):
        for s in range(2):
            for k in range(NY):
                n = (2 * w + s) * NY + k
                copies.append(
                    pltpu.make_async_copy(
                        arrays[k].at[pl.ds((2 + s) * rows, rows)],
                        cot_buf.at[2 * w + s, pl.ds(k * rows, rows)],
                        sems.at[n],
                    )
                )
                copies[-1].start()
    for j in range(NZ):
        place = ((y - j) & 3) * rows
        att_scr[:, pl.ds(pl.multiple_of(place, 128), rows)] = att_ref[j]
    for w in range(2):
        for s in range(2):
            for copy in copies[(2 * w + s) * NY : (2 * w + s + 1) * NY]:
                copy.wait()
            acc = dot_nn(att_scr[...], cot_buf[2 * w + s])
            target = (((zl ^ s) * 2 + (c ^ w)) - x) & 3

            for n in range(NX):

                @pl.when(target == n)
                def _(n=n, acc=acc):
                    outs[n][...] = acc.astype(outs[n].dtype)


def per_device(
    queries,
    local_keys,
    local_values,
    segments,
    memory_keys,
    memory_values,
    retrieved,
    block_slot,
    gate_bias,
    out_weight,
    cotangent,
):
    rows, width = queries.shape
    heads = width // HEAD
    mem, ten = lax.axis_index("mem"), lax.axis_index("tensor")
    z, x = mem // NX, mem % NX
    y, zl, c = ten // 4, (ten // 2) % 2, ten % 2
    ids = jnp.stack([z, x, y, jnp.zeros_like(z), zl, c]).astype(jnp.int32)
    gate = jax.nn.sigmoid(gate_bias)
    params = pltpu.CompilerParams(vmem_limit_bytes=16 << 20)

    names = jnp.arange(block_slot.shape[0], dtype=jnp.int32)
    storage = jnp.sum(
        jnp.where(retrieved.reshape(-1)[:, None] == names[None, :], block_slot[None, :], 0), axis=1
    )
    extra = jnp.zeros((EXTRA, width), jnp.bfloat16)
    extra = extra.at[0, 0 : storage.shape[0]].set(storage.astype(jnp.bfloat16))
    q_pack = jnp.concatenate([queries, extra], axis=0)

    q_all = exchange_z(jnp.broadcast_to(q_pack[None], (NZ, *q_pack.shape)))
    k1, v3, v1, k3, swapped = together(
        shift_x(memory_keys, 1),
        shift_x(memory_values, -1),
        shift_x(memory_values, 1),
        shift_x(memory_keys, -1),
        swap_zy(cotangent),
    )
    both = jnp.concatenate([cotangent, swapped], axis=0)
    k2, v2, pair = shift_x(k1, 1), shift_x(v3, -1), flip_tensor(both, 2)
    quad = jnp.concatenate([both[:rows], pair[:rows], both[rows:], pair[rows:]], axis=0)

    stored = q_all[:, rows, 0:16].astype(jnp.int32).reshape(8, 8)
    shards = z * NX + (x - jnp.arange(NX, dtype=jnp.int32)) % NX
    hit = (stored // SLOTS)[:, None, :] == shards[None, :, None]
    sel = (jnp.sum(jnp.where(hit, (stored % SLOTS)[:, None, :] + 1, 0), axis=2) - 1).reshape(-1)

    local_out = pl.pallas_call(
        local_kernel,
        out_shape=jax.ShapeDtypeStruct((rows, width), jnp.float32),
        in_specs=[SM] + [VM] * 4,
        out_specs=VM,
        compiler_params=params,
        name="local_attention",
    )(gate, segments.reshape(1, rows), queries, local_keys, local_values)

    k2, v2, quad = together(k2, v2, quad)
    parts = pl.pallas_call(
        memory_kernel,
        out_shape=jax.ShapeDtypeStruct((NZ, rows + EXTRA, width), jnp.bfloat16),
        in_specs=[SM] + [HB] * 9,
        out_specs=VM,
        scratch_shapes=[
            pltpu.VMEM((NZ, rows + EXTRA, width), jnp.bfloat16),
            pltpu.VMEM((NX, SLOTS * BLOCK, width), jnp.bfloat16),
            pltpu.VMEM((NX, SLOTS * BLOCK, width), jnp.bfloat16),
            pltpu.SemaphoreType.DMA((9,)),
        ],
        compiler_params=params,
        name="memory_attention",
    )(sel, q_all, memory_keys, k1, k2, k3, memory_values, v1, v2, v3)

    back = exchange_z(parts)
    attention, att_t = pl.pallas_call(
        merge_kernel,
        out_shape=[
            jax.ShapeDtypeStruct((rows, width), jnp.bfloat16),
            jax.ShapeDtypeStruct((NZ, width, rows), jnp.bfloat16),
        ],
        in_specs=[SM] + [VM] * 2,
        out_specs=[VM] * 2,
        compiler_params=params,
        name="merge",
    )(gate, local_out, back)
    att_all = exchange_z(att_t)

    y1, y2, y3 = [shift_y(quad, k) for k in (1, 2, 3)]
    c0, c1, c2, c3 = [flip_tensor(v, 1) for v in (quad, y1, y2, y3)]
    own, other = [quad, y1, y2, y3], [c0, c1, c2, c3]

    attention_grad = pl.pallas_call(
        grad_kernel,
        out_shape=jax.ShapeDtypeStruct((rows, width), jnp.bfloat16),
        grid_spec=pltpu.PrefetchScalarGridSpec(
            num_scalar_prefetch=1,
            grid=(NY,),
            in_specs=[
                pl.BlockSpec(
                    (4 * rows, width), lambda g, ids: (0, 0), pipeline_mode=pl.Buffered(1)
                )
            ]
            * 8
            + [pl.BlockSpec((width, 4 * width), lambda g, ids: (0, (ids[2] - g) & 3))],
            out_specs=pl.BlockSpec((rows, width), lambda g, ids: (0, 0)),
            scratch_shapes=[pltpu.VMEM((rows, width), jnp.float32)],
        ),
        compiler_params=params,
        name="attention_grad",
    )(ids, *own, *other, *in_hbm([out_weight]))

    mine, *sent = pl.pallas_call(
        weight_kernel,
        out_shape=[jax.ShapeDtypeStruct((width, width), jnp.float32)]
        + [jax.ShapeDtypeStruct((width, width), jnp.bfloat16)] * 3,
        in_specs=[SM, VM] + [HB] * 8,
        out_specs=[VM] * 4,
        scratch_shapes=[
            pltpu.VMEM((width, NZ * rows), jnp.bfloat16),
            pltpu.VMEM((4, NY * rows, width), jnp.bfloat16),
            pltpu.SemaphoreType.DMA((16,)),
        ],
        compiler_params=params,
        name="weight_partials",
    )(ids, att_all, *own, *other)
    got = [shift_x(sent[n - 1], n) for n in (1, 2, 3)]
    weight_grad = (mine + got[0].astype(jnp.float32)) + (
        got[1].astype(jnp.float32) + got[2].astype(jnp.float32)
    )
    return (attention, attention_grad, weight_grad)


def solution(mesh):
    return jax.shard_map(
        per_device,
        mesh=mesh,
        in_specs=(
            P("mem", "tensor"),
            P("mem", "tensor"),
            P("mem", "tensor"),
            P("mem"),
            P("mem", "tensor"),
            P("mem", "tensor"),
            P("mem", None),
            P(),
            P("tensor"),
            P("tensor", None),
            P("mem", "tensor"),
        ),
        out_specs=(P("mem", "tensor"), P("mem", "tensor"), P("tensor", "mem")),
        check_vma=False,
    )
```

```python
import jax
import jax.numpy as jnp
from jax import lax
from jax.experimental import pallas as pl
from jax.experimental.pallas import tpu as pltpu
from jax.sharding import PartitionSpec as P

HEAD = 128
BLOCK = 128
SLOTS = 4
NX = 4
NZ = 4
NY = 4
LOG2E = 1.4426950408889634
SCALE2 = HEAD**-0.5 * LOG2E
NEG = -1e30
EXTRA = 16

VM = pl.BlockSpec(memory_space=pltpu.VMEM)
SM = pl.BlockSpec(memory_space=pltpu.SMEM)
HB = pl.BlockSpec(memory_space=pltpu.HBM)


def cost(flops, transcendentals, bytes_accessed):
    return pl.CostEstimate(
        flops=flops, transcendentals=transcendentals, bytes_accessed=bytes_accessed
    )


def in_hbm(values):
    return [pltpu.with_memory_space_constraint(v, pltpu.HBM) for v in values]


def together(*values):
    return lax.optimization_barrier(values)


def after(value, *deps):
    return lax.optimization_barrier((value, *deps))[0]


def dot_nt(a, b):
    return lax.dot_general(a, b, (((1,), (1,)), ((), ())), preferred_element_type=jnp.float32)


def dot_nn(a, b):
    return lax.dot_general(a, b, (((1,), (0,)), ((), ())), preferred_element_type=jnp.float32)


def shift_x(value, k):
    pairs = [(z * NX + x, z * NX + (x + k) % NX) for z in range(NZ) for x in range(NX)]
    return lax.ppermute(value, "mem", pairs)


def shift_z(value, k):
    pairs = [(z * NX + x, (z + k) % NZ * NX + x) for z in range(NZ) for x in range(NX)]
    return lax.ppermute(value, "mem", pairs)


def exchange_z(value):
    groups = [[z * NX + x for z in range(NZ)] for x in range(NX)]
    return lax.all_to_all(
        value, "mem", split_axis=0, concat_axis=0, axis_index_groups=groups, tiled=True
    )


def shift_y(value, k):
    pairs = [(y * 4 + r, (y + k) % NY * 4 + r) for y in range(NY) for r in range(4)]
    return lax.ppermute(value, "tensor", pairs)


def gather_y(value):
    return [value] + [shift_y(value, k) for k in (1, 2, 3)]


def flip_tensor(value, bit):
    return lax.ppermute(value, "tensor", [(t, t ^ bit) for t in range(16)])


def swap_zy(value):
    pairs = []
    for z in range(NZ):
        for x in range(NX):
            for y in range(NY):
                for r in range(4):
                    pairs.append(((z * NX + x) * 16 + y * 4 + r, (y * NX + x) * 16 + z * 4 + r))
    return lax.ppermute(value, ("mem", "tensor"), pairs)


def local_kernel(gate_ref, seg_ref, q_ref, k_ref, v_ref, out_ref):
    rows = q_ref.shape[0]
    heads = q_ref.shape[1] // HEAD
    seg_cols = jnp.broadcast_to(seg_ref[...].astype(jnp.float32), (rows, rows))
    seg_rows = seg_cols.T
    row_ids = lax.broadcasted_iota(jnp.int32, (rows, rows), 0)
    col_ids = lax.broadcasted_iota(jnp.int32, (rows, rows), 1)
    allowed = (col_ids <= row_ids) & (seg_cols == seg_rows)
    for h in range(heads):
        cols = pl.ds(h * HEAD, HEAD)
        scores = jnp.where(allowed, dot_nt(q_ref[:, cols], k_ref[:, cols]) * SCALE2, NEG)
        top = jnp.max(scores, axis=1, keepdims=True)
        weights = jnp.exp2(scores - top)
        total = jnp.sum(weights, axis=1, keepdims=True)
        out = dot_nn(weights.astype(jnp.bfloat16), v_ref[:, cols])
        out_ref[:, cols] = out * ((1.0 - gate_ref[h]) / total)


def memory_kernel(ids_ref, stored_ref, *refs):
    sources, result_ref = refs[0:12], refs[12]
    q_buf, k_buf, v_buf, sel_ref, sems = refs[13:18]
    targets = [buf.at[n] for buf in (q_buf, k_buf, v_buf) for n in range(4)]
    copies = [
        pltpu.make_async_copy(src, dst, sems.at[n])
        for n, (src, dst) in enumerate(zip(sources, targets))
    ]
    for copy in copies:
        copy.start()

    z, x = ids_ref[0], ids_ref[1]
    for n in range(2 * NZ * NX):
        sel_ref[n] = -1
    for n in range(2 * NZ * 8):
        block = stored_ref[n]
        shard = block // SLOTS
        place = n // 8 * NX + ((x - shard) & 3)
        sel_ref[jnp.where(shard // NX == z, place, 2 * NZ * NX)] = block % SLOTS

    for copy in copies:
        copy.wait()
    q_refs, k_refs, v_refs = [[buf.at[n] for n in range(4)] for buf in (q_buf, k_buf, v_buf)]
    heads = k_buf.shape[2] // HEAD
    lane = lax.broadcasted_iota(jnp.int32, (BLOCK, BLOCK), 1)
    for j in range(NZ):
        q_ref, out_ref = q_refs[j], result_ref.at[(z - j) & 3]

        for b in range(2):
            row = b * BLOCK
            stat = jnp.zeros((BLOCK, BLOCK), jnp.float32)
            starts, biases = [], []
            for i in range(NX):
                slot = sel_ref[(2 * j + b) * NX + i]
                starts.append(pl.multiple_of(jnp.maximum(slot, 0) * BLOCK, BLOCK))
                biases.append(
                    jnp.full((1, BLOCK), jnp.where(slot >= 0, 0.0, NEG), jnp.float32)
                )
            bias = jnp.concatenate(biases, axis=1)
            for h in range(heads):
                cols = pl.ds(h * HEAD, HEAD)
                query = q_ref[pl.ds(row, BLOCK), cols]
                keys = jnp.concatenate([k_refs[i][pl.ds(starts[i], BLOCK), cols] for i in range(NX)])
                values = jnp.concatenate(
                    [v_refs[i][pl.ds(starts[i], BLOCK), cols] for i in range(NX)]
                )
                scores = dot_nt(query, keys) * SCALE2 + bias
                top = jnp.max(scores, axis=1, keepdims=True)
                weights = jnp.exp2(scores - top)
                total = jnp.sum(weights, axis=1, keepdims=True)
                acc = dot_nn(weights.astype(jnp.bfloat16), values)
                out_ref[pl.ds(row, BLOCK), cols] = (acc / total).astype(jnp.bfloat16)
                stat = jnp.where(lane == h, top + jnp.log2(total), stat)
            stat = stat.T[0:8]
            high = stat.astype(jnp.bfloat16)
            rest = stat - high.astype(jnp.float32)
            mid = rest.astype(jnp.bfloat16)
            low = rest - mid.astype(jnp.float32)
            packed = jnp.concatenate(
                [
                    high[0:4].astype(jnp.float32),
                    mid[0:4].astype(jnp.float32),
                    low[0:4],
                    jnp.zeros((4, BLOCK), jnp.float32),
                ],
                axis=0,
            )
            out_ref[2 * BLOCK : 2 * BLOCK + EXTRA, pl.ds(row, BLOCK)] = packed.astype(jnp.bfloat16)
        out_ref[2 * BLOCK : 2 * BLOCK + EXTRA, 2 * BLOCK :] = jnp.zeros(
            (EXTRA, out_ref.shape[1] - 2 * BLOCK), jnp.bfloat16
        )


def merge_kernel(gate_ref, local_ref, back_ref, att_ref, att_t_ref):
    parts = [back_ref.at[n] for n in range(NZ)]
    heads = local_ref.shape[1] // HEAD
    for b in range(2):
        rows = pl.ds(b * BLOCK, BLOCK)
        logs = []
        for p in parts:
            s = p[2 * BLOCK : 2 * BLOCK + EXTRA, rows].astype(jnp.float32)
            logs.append((s[0:4] + s[4:8]) + s[8:12])
        top = jnp.maximum(jnp.maximum(logs[0], logs[1]), jnp.maximum(logs[2], logs[3]))
        shares = [jnp.exp2(s - top) for s in logs]
        total = (shares[0] + shares[1]) + (shares[2] + shares[3])
        shares = [s / total for s in shares]
        table = jnp.concatenate(shares + [jnp.zeros((BLOCK - 16, BLOCK), jnp.float32)], axis=0).T
        for h in range(heads):
            cols = pl.ds(h * HEAD, HEAD)
            acc = None
            for n, p in enumerate(parts):
                term = p[rows, cols].astype(jnp.float32) * table[:, 4 * n + h : 4 * n + h + 1]
                acc = term if acc is None else acc + term
            out = gate_ref[h] * acc + local_ref[rows, cols]
            att_ref[rows, cols] = out.astype(jnp.bfloat16)
            flipped = out.T.astype(jnp.bfloat16)
            for n in range(NZ):
                att_t_ref[n, cols, rows] = flipped


def grad_kernel(ids_ref, *refs):
    own, other, w_ref, out_ref, acc_ref = refs[0:4], refs[4:8], refs[8], refs[9], refs[10]
    step = pl.program_id(0)
    zl, c = ids_ref[4], ids_ref[5]
    width = own[0].shape[1]
    rows = out_ref.shape[0]

    @pl.when(step == 0)
    def _():
        acc_ref[...] = jnp.zeros_like(acc_ref)

    for k in range(NY):

        @pl.when(step == k)
        def _(k=k):
            acc = acc_ref[...]
            for w, arrays in enumerate((own, other)):
                for s in range(2):
                    place = (zl ^ s) * 2 + (c ^ w)
                    cols = pl.ds(pl.multiple_of(place * width, 128), width)
                    acc = acc + dot_nt(arrays[k][s * rows : (s + 1) * rows, :], w_ref[:, cols])
            acc_ref[...] = acc

    @pl.when(step == NY - 1)
    def _():
        out_ref[...] = acc_ref[...].astype(jnp.bfloat16)


def weight_kernel(ids_ref, *refs):
    att_ref, own, other = refs[0], refs[1:5], refs[5:9]
    outs, att_scr, cot_buf, sems = refs[9:13], refs[13], refs[14], refs[15]
    x, y, zl, c = ids_ref[1], ids_ref[2], ids_ref[4], ids_ref[5]
    rows = att_ref.shape[2]
    copies = []
    for w, arrays in enumerate((own, other)):
        for s in range(2):
            for k in range(NY):
                n = (2 * w + s) * NY + k
                copies.append(
                    pltpu.make_async_copy(
                        arrays[k].at[pl.ds(s * rows, rows)],
                        cot_buf.at[2 * w + s, pl.ds(k * rows, rows)],
                        sems.at[n],
                    )
                )
                copies[-1].start()
    for j in range(NZ):
        place = ((y - j) & 3) * rows
        att_scr[:, pl.ds(pl.multiple_of(place, 128), rows)] = att_ref[j]
    for w in range(2):
        for s in range(2):
            for copy in copies[(2 * w + s) * NY : (2 * w + s + 1) * NY]:
                copy.wait()
            acc = dot_nn(att_scr[...], cot_buf[2 * w + s])
            target = (((zl ^ s) * 2 + (c ^ w)) - x) & 3

            for n in range(NX):

                @pl.when(target == n)
                def _(n=n, acc=acc):
                    outs[n][...] = acc.astype(outs[n].dtype)


def per_device(
    queries,
    local_keys,
    local_values,
    segments,
    memory_keys,
    memory_values,
    retrieved,
    block_slot,
    gate_bias,
    out_weight,
    cotangent,
):
    rows, width = queries.shape
    heads = width // HEAD
    mem, ten = lax.axis_index("mem"), lax.axis_index("tensor")
    z, x = mem // NX, mem % NX
    y, zl, c = ten // 4, (ten // 2) % 2, ten % 2
    ids = jnp.stack([z, x, y, jnp.zeros_like(z), zl, c]).astype(jnp.int32)
    gate = jax.nn.sigmoid(gate_bias)
    params = pltpu.CompilerParams(vmem_limit_bytes=16 << 20)

    names = jnp.arange(block_slot.shape[0], dtype=jnp.int32)
    storage = jnp.sum(
        jnp.where(retrieved.reshape(-1)[:, None] == names[None, :], block_slot[None, :], 0), axis=1
    )
    extra = jnp.zeros((EXTRA, width), jnp.bfloat16)
    extra = extra.at[0, 0 : storage.shape[0]].set(storage.astype(jnp.bfloat16))
    q_pack = jnp.concatenate([queries, extra], axis=0)

    k1, v3 = shift_x(memory_keys, 1), shift_x(memory_values, -1)
    q1, q3 = shift_z(q_pack, 1), shift_z(q_pack, 3)
    near = flip_tensor(cotangent, 2)
    k1, v3, q1, q3, near, own_keys, own_values, q_late = together(
        k1, v3, q1, q3, near, memory_keys, memory_values, q_pack
    )
    k2, v2, q2 = shift_x(k1, 1), shift_x(v3, -1), shift_z(q_late, 2)
    k3, v1 = shift_x(own_keys, -1), shift_x(own_values, 1)
    k2, v2, k3, v1, q2, near = together(k2, v2, k3, v1, q2, near)
    pair = jnp.concatenate([cotangent, near], axis=0)
    w1, w3, swapped = shift_y(pair, 1), shift_y(pair, 3), swap_zy(pair[:rows])
    q_all = [q_pack, q1, q2, q3]
    stored = jnp.stack([q[rows, 0:16] for q in q_all]).reshape(-1).astype(jnp.int32)

    local_out = pl.pallas_call(
        local_kernel,
        out_shape=jax.ShapeDtypeStruct((rows, width), jnp.float32),
        in_specs=[SM] + [VM] * 4,
        out_specs=VM,
        compiler_params=params,
        cost_estimate=cost(4 * heads * rows * rows * HEAD, heads * rows * rows, 6 * rows * width),
        name="local_attention",
    )(gate, segments.reshape(1, rows), queries, local_keys, local_values)

    parts = pl.pallas_call(
        memory_kernel,
        out_shape=jax.ShapeDtypeStruct((NZ, rows + EXTRA, width), jnp.bfloat16),
        in_specs=[SM] * 2 + [HB] * 12,
        out_specs=VM,
        scratch_shapes=[
            pltpu.VMEM((NZ, rows + EXTRA, width), jnp.bfloat16),
            pltpu.VMEM((NX, SLOTS * BLOCK, width), jnp.bfloat16),
            pltpu.VMEM((NX, SLOTS * BLOCK, width), jnp.bfloat16),
            pltpu.SMEM((2 * NZ * NX + 1,), jnp.int32),
            pltpu.SemaphoreType.DMA((12,)),
        ],
        compiler_params=params,
        cost_estimate=cost(
            64 * heads * rows * rows * HEAD, 8 * heads * rows * rows, 24 * rows * width
        ),
        name="memory_attention",
    )(ids, stored, *in_hbm([*q_all, memory_keys, k1, k2, k3, memory_values, v1, v2, v3]))

    parts, swapped, w1, w3, pair = together(parts, swapped, w1, w3, pair)
    back = exchange_z(parts)
    tall = jnp.concatenate([swapped, flip_tensor(swapped, 2)], axis=0)
    w2, t1, t3 = shift_y(pair, 2), shift_y(tall, 1), shift_y(tall, 3)
    back, w2, t1, t3, tall = together(back, w2, t1, t3, tall)
    attention, att_t = pl.pallas_call(
        merge_kernel,
        out_shape=[
            jax.ShapeDtypeStruct((rows, width), jnp.bfloat16),
            jax.ShapeDtypeStruct((NZ, width, rows), jnp.bfloat16),
        ],
        in_specs=[SM] + [VM] * 2,
        out_specs=[VM] * 2,
        compiler_params=params,
        cost_estimate=cost(32 * rows * width, 4 * rows, 16 * rows * width),
        name="merge",
    )(gate, local_out, back)
    att_t, tall, pair = together(att_t, tall, pair)
    att_all = exchange_z(att_t)
    t2 = shift_y(tall, 2)
    tall = [tall, t1, t2, t3]
    tall = tall + [flip_tensor(v, 1) for v in tall]
    wide = [pair, w1, w2, w3]
    wide = wide + [flip_tensor(v, 1) for v in wide]
    att_all, *flipped = together(att_all, *tall[4:], *wide[4:])
    tall, wide = in_hbm(tall[:4] + flipped[:4]), in_hbm(wide[:4] + flipped[4:])

    attention_grad = pl.pallas_call(
        grad_kernel,
        out_shape=jax.ShapeDtypeStruct((rows, width), jnp.bfloat16),
        grid_spec=pltpu.PrefetchScalarGridSpec(
            num_scalar_prefetch=1,
            grid=(NY,),
            in_specs=[
                pl.BlockSpec(
                    (2 * rows, width), lambda g, ids: (0, 0), pipeline_mode=pl.Buffered(1)
                )
            ]
            * 8
            + [pl.BlockSpec((width, 4 * width), lambda g, ids: (0, (ids[2] - g) & 3))],
            out_specs=pl.BlockSpec((rows, width), lambda g, ids: (0, 0)),
            scratch_shapes=[pltpu.VMEM((rows, width), jnp.float32)],
        ),
        compiler_params=params,
        cost_estimate=cost(32 * rows * width * width, 0, 64 * rows * width),
        name="attention_grad",
    )(ids, *wide, *in_hbm([out_weight]))

    mine, *sent = pl.pallas_call(
        weight_kernel,
        out_shape=[jax.ShapeDtypeStruct((width, width), jnp.float32)]
        + [jax.ShapeDtypeStruct((width, width), jnp.bfloat16)] * 3,
        in_specs=[SM, VM] + [HB] * 8,
        out_specs=[VM] * 4,
        scratch_shapes=[
            pltpu.VMEM((width, NZ * rows), jnp.bfloat16),
            pltpu.VMEM((4, NY * rows, width), jnp.bfloat16),
            pltpu.SemaphoreType.DMA((16,)),
        ],
        compiler_params=params,
        cost_estimate=cost(32 * rows * width * width, 0, 48 * rows * width),
        name="weight_partials",
    )(ids, att_all, *tall)
    got = [shift_x(sent[n - 1], n) for n in (1, 2, 3)]
    weight_grad = (mine + got[0].astype(jnp.float32)) + (
        got[1].astype(jnp.float32) + got[2].astype(jnp.float32)
    )
    return (attention, attention_grad, weight_grad)


def solution(mesh):
    return jax.shard_map(
        per_device,
        mesh=mesh,
        in_specs=(
            P("mem", "tensor"),
            P("mem", "tensor"),
            P("mem", "tensor"),
            P("mem"),
            P("mem", "tensor"),
            P("mem", "tensor"),
            P("mem", None),
            P(),
            P("tensor"),
            P("tensor", None),
            P("mem", "tensor"),
        ),
        out_specs=(P("mem", "tensor"), P("mem", "tensor"), P("tensor", "mem")),
        check_vma=False,
    )
```

```python
import jax
import jax.numpy as jnp
from jax import lax
from jax.experimental import pallas as pl
from jax.experimental.pallas import tpu as pltpu
from jax.sharding import PartitionSpec as P

HEAD = 128
BLOCK = 128
SLOTS = 4
NX = 4
NZ = 4
NY = 4
LOG2E = 1.4426950408889634
SCALE2 = HEAD**-0.5 * LOG2E
NEG = -1e30
EXTRA = 16

VM = pl.BlockSpec(memory_space=pltpu.VMEM)
SM = pl.BlockSpec(memory_space=pltpu.SMEM)
HB = pl.BlockSpec(memory_space=pltpu.HBM)


def cost(flops, transcendentals, bytes_accessed):
    return pl.CostEstimate(
        flops=flops, transcendentals=transcendentals, bytes_accessed=bytes_accessed
    )


def in_hbm(values):
    return [pltpu.with_memory_space_constraint(v, pltpu.HBM) for v in values]


def together(*values):
    return lax.optimization_barrier(values)


def after(value, *deps):
    return lax.optimization_barrier((value, *deps))[0]


def dot_nt(a, b):
    return lax.dot_general(a, b, (((1,), (1,)), ((), ())), preferred_element_type=jnp.float32)


def dot_nn(a, b):
    return lax.dot_general(a, b, (((1,), (0,)), ((), ())), preferred_element_type=jnp.float32)


def shift_x(value, k):
    pairs = [(z * NX + x, z * NX + (x + k) % NX) for z in range(NZ) for x in range(NX)]
    return lax.ppermute(value, "mem", pairs)


def shift_z(value, k):
    pairs = [(z * NX + x, (z + k) % NZ * NX + x) for z in range(NZ) for x in range(NX)]
    return lax.ppermute(value, "mem", pairs)


def exchange_z(value):
    groups = [[z * NX + x for z in range(NZ)] for x in range(NX)]
    return lax.all_to_all(
        value, "mem", split_axis=0, concat_axis=0, axis_index_groups=groups, tiled=True
    )


def shift_y(value, k):
    pairs = [(y * 4 + r, (y + k) % NY * 4 + r) for y in range(NY) for r in range(4)]
    return lax.ppermute(value, "tensor", pairs)


def gather_y(value):
    return [value] + [shift_y(value, k) for k in (1, 2, 3)]


def flip_tensor(value, bit):
    return lax.ppermute(value, "tensor", [(t, t ^ bit) for t in range(16)])


def swap_zy(value):
    pairs = []
    for z in range(NZ):
        for x in range(NX):
            for y in range(NY):
                for r in range(4):
                    pairs.append(((z * NX + x) * 16 + y * 4 + r, (y * NX + x) * 16 + z * 4 + r))
    return lax.ppermute(value, ("mem", "tensor"), pairs)


def local_kernel(gate_ref, seg_ref, q_ref, k_ref, v_ref, out_ref):
    rows = q_ref.shape[0]
    heads = q_ref.shape[1] // HEAD
    seg_cols = jnp.broadcast_to(seg_ref[...].astype(jnp.float32), (rows, rows))
    seg_rows = seg_cols.T
    row_ids = lax.broadcasted_iota(jnp.int32, (rows, rows), 0)
    col_ids = lax.broadcasted_iota(jnp.int32, (rows, rows), 1)
    allowed = (col_ids <= row_ids) & (seg_cols == seg_rows)
    for h in range(heads):
        cols = pl.ds(h * HEAD, HEAD)
        scores = jnp.where(allowed, dot_nt(q_ref[:, cols], k_ref[:, cols]) * SCALE2, NEG)
        top = jnp.max(scores, axis=1, keepdims=True)
        weights = jnp.exp2(scores - top)
        total = jnp.sum(weights, axis=1, keepdims=True)
        out = dot_nn(weights.astype(jnp.bfloat16), v_ref[:, cols])
        out_ref[:, cols] = out * ((1.0 - gate_ref[h]) / total)


def memory_kernel(ids_ref, stored_ref, *refs):
    sources, result_ref = refs[0:12], refs[12]
    q_buf, k_buf, v_buf, sel_ref, sems = refs[13:18]
    targets = [buf.at[n] for buf in (q_buf, k_buf, v_buf) for n in range(4)]
    copies = [
        pltpu.make_async_copy(src, dst, sems.at[n])
        for n, (src, dst) in enumerate(zip(sources, targets))
    ]
    for copy in copies:
        copy.start()

    z, x = ids_ref[0], ids_ref[1]
    for n in range(2 * NZ * NX):
        sel_ref[n] = -1
    for n in range(2 * NZ * 8):
        block = stored_ref[n]
        shard = block // SLOTS
        place = n // 8 * NX + ((x - shard) & 3)
        sel_ref[jnp.where(shard // NX == z, place, 2 * NZ * NX)] = block % SLOTS

    for copy in copies[4:8] + copies[0:4]:
        copy.wait()
    q_refs, k_refs, v_refs = [[buf.at[n] for n in range(4)] for buf in (q_buf, k_buf, v_buf)]
    heads = k_buf.shape[2] // HEAD
    lane = lax.broadcasted_iota(jnp.int32, (BLOCK, BLOCK), 1)
    for j in range(NZ):
        q_ref, out_ref = q_refs[j], result_ref.at[(z - j) & 3]

        for b in range(2):
            row = b * BLOCK
            stat = jnp.zeros((BLOCK, BLOCK), jnp.float32)
            starts, biases = [], []
            for i in range(NX):
                slot = sel_ref[(2 * j + b) * NX + i]
                starts.append(pl.multiple_of(jnp.maximum(slot, 0) * BLOCK, BLOCK))
                biases.append(
                    jnp.full((1, BLOCK), jnp.where(slot >= 0, 0.0, NEG), jnp.float32)
                )
            bias = jnp.concatenate(biases, axis=1)
            for h in range(heads):
                cols = pl.ds(h * HEAD, HEAD)
                query = q_ref[pl.ds(row, BLOCK), cols]
                keys = jnp.concatenate([k_refs[i][pl.ds(starts[i], BLOCK), cols] for i in range(NX)])
                scores = dot_nt(query, keys) * SCALE2 + bias
                top = jnp.max(scores, axis=1, keepdims=True)
                weights = jnp.exp2(scores - top)
                total = jnp.sum(weights, axis=1, keepdims=True)
                if (j, b, h) == (0, 0, 0):
                    for copy in copies[8:12]:
                        copy.wait()
                values = jnp.concatenate(
                    [v_refs[i][pl.ds(starts[i], BLOCK), cols] for i in range(NX)]
                )
                acc = dot_nn(weights.astype(jnp.bfloat16), values)
                out_ref[pl.ds(row, BLOCK), cols] = (acc / total).astype(jnp.bfloat16)
                stat = jnp.where(lane == h, top + jnp.log2(total), stat)
            stat = stat.T[0:8]
            high = stat.astype(jnp.bfloat16)
            rest = stat - high.astype(jnp.float32)
            mid = rest.astype(jnp.bfloat16)
            low = rest - mid.astype(jnp.float32)
            packed = jnp.concatenate(
                [
                    high[0:4].astype(jnp.float32),
                    mid[0:4].astype(jnp.float32),
                    low[0:4],
                    jnp.zeros((4, BLOCK), jnp.float32),
                ],
                axis=0,
            )
            out_ref[2 * BLOCK : 2 * BLOCK + EXTRA, pl.ds(row, BLOCK)] = packed.astype(jnp.bfloat16)
        out_ref[2 * BLOCK : 2 * BLOCK + EXTRA, 2 * BLOCK :] = jnp.zeros(
            (EXTRA, out_ref.shape[1] - 2 * BLOCK), jnp.bfloat16
        )


def merge_kernel(gate_ref, local_ref, back_ref, att_ref, att_t_ref):
    parts = [back_ref.at[n] for n in range(NZ)]
    heads = local_ref.shape[1] // HEAD
    for b in range(2):
        rows = pl.ds(b * BLOCK, BLOCK)
        logs = []
        for p in parts:
            s = p[2 * BLOCK : 2 * BLOCK + EXTRA, rows].astype(jnp.float32)
            logs.append((s[0:4] + s[4:8]) + s[8:12])
        top = jnp.maximum(jnp.maximum(logs[0], logs[1]), jnp.maximum(logs[2], logs[3]))
        shares = [jnp.exp2(s - top) for s in logs]
        total = (shares[0] + shares[1]) + (shares[2] + shares[3])
        shares = [s / total for s in shares]
        table = jnp.concatenate(shares + [jnp.zeros((BLOCK - 16, BLOCK), jnp.float32)], axis=0).T
        for h in range(heads):
            cols = pl.ds(h * HEAD, HEAD)
            acc = None
            for n, p in enumerate(parts):
                term = p[rows, cols].astype(jnp.float32) * table[:, 4 * n + h : 4 * n + h + 1]
                acc = term if acc is None else acc + term
            out = gate_ref[h] * acc + local_ref[rows, cols]
            att_ref[rows, cols] = out.astype(jnp.bfloat16)
            flipped = out.T.astype(jnp.bfloat16)
            for n in range(NZ):
                att_t_ref[n, cols, rows] = flipped


def grad_kernel(ids_ref, *refs):
    tall, w_ref, out_ref = refs[0:8], refs[8], refs[9]
    cot_buf, w_buf, sems = refs[10:13]
    z, y, zl, c = ids_ref[0], ids_ref[2], ids_ref[4], ids_ref[5]
    rows, width = out_ref.shape[1], out_ref.shape[2]
    copies = []
    for w in range(2):
        for s in range(2):
            column = (z * 4 + (zl ^ s) * 2 + (c ^ w)) * width
            part = pl.ds((2 * w + s) * width, width)
            copies.append(
                pltpu.make_async_copy(
                    w_ref.at[:, pl.ds(pl.multiple_of(column, 128), width)],
                    w_buf.at[:, part],
                    sems.at[2 * w + s],
                )
            )
    for k in range(NY):
        for w in range(2):
            for s in range(2):
                copies.append(
                    pltpu.make_async_copy(
                        tall[NY * w + k].at[pl.ds(s * rows, rows)],
                        cot_buf.at[k, :, pl.ds((2 * w + s) * width, width)],
                        sems.at[4 * (k + 1) + 2 * w + s],
                    )
                )
    for copy in copies:
        copy.start()
    for copy in copies[:4]:
        copy.wait()
    for k in range(NY):
        for copy in copies[4 * (k + 1) : 4 * (k + 2)]:
            copy.wait()
        out_ref[(y - k) & 3] = dot_nt(cot_buf[k], w_buf[...]).astype(jnp.bfloat16)


def weight_kernel(ids_ref, *refs):
    att_ref, own, other = refs[0], refs[1:5], refs[5:9]
    outs, att_scr, cot_buf, sems = refs[9:13], refs[13], refs[14], refs[15]
    x, y, zl, c = ids_ref[1], ids_ref[2], ids_ref[4], ids_ref[5]
    rows = att_ref.shape[2]
    copies = []
    for w, arrays in enumerate((own, other)):
        for s in range(2):
            for k in range(NY):
                n = (2 * w + s) * NY + k
                copies.append(
                    pltpu.make_async_copy(
                        arrays[k].at[pl.ds(s * rows, rows)],
                        cot_buf.at[2 * w + s, pl.ds(k * rows, rows)],
                        sems.at[n],
                    )
                )
                copies[-1].start()
    for j in range(NZ):
        place = ((y - j) & 3) * rows
        att_scr[:, pl.ds(pl.multiple_of(place, 128), rows)] = att_ref[j]
    for w in range(2):
        for s in range(2):
            for copy in copies[(2 * w + s) * NY : (2 * w + s + 1) * NY]:
                copy.wait()
            acc = dot_nn(att_scr[...], cot_buf[2 * w + s])
            target = (((zl ^ s) * 2 + (c ^ w)) - x) & 3

            for n in range(NX):

                @pl.when(target == n)
                def _(n=n, acc=acc):
                    outs[n][...] = acc.astype(outs[n].dtype)


def per_device(
    queries,
    local_keys,
    local_values,
    segments,
    memory_keys,
    memory_values,
    retrieved,
    block_slot,
    gate_bias,
    out_weight,
    cotangent,
):
    rows, width = queries.shape
    heads = width // HEAD
    mem, ten = lax.axis_index("mem"), lax.axis_index("tensor")
    z, x = mem // NX, mem % NX
    y, zl, c = ten // 4, (ten // 2) % 2, ten % 2
    ids = jnp.stack([z, x, y, jnp.zeros_like(z), zl, c]).astype(jnp.int32)
    gate = jax.nn.sigmoid(gate_bias)
    params = pltpu.CompilerParams(vmem_limit_bytes=16 << 20)

    names = jnp.arange(block_slot.shape[0], dtype=jnp.int32)
    storage = jnp.sum(
        jnp.where(retrieved.reshape(-1)[:, None] == names[None, :], block_slot[None, :], 0), axis=1
    )
    extra = jnp.zeros((EXTRA, width), jnp.bfloat16)
    extra = extra.at[0, 0 : storage.shape[0]].set(storage.astype(jnp.bfloat16))
    q_pack = jnp.concatenate([queries, extra], axis=0)

    swapped = swap_zy(cotangent)
    k1, v3 = shift_x(memory_keys, 1), shift_x(memory_values, -1)
    q1, q3 = shift_z(q_pack, 1), shift_z(q_pack, 3)
    k2, v2 = shift_x(k1, 1), shift_x(v3, -1)
    v1, k3 = shift_x(after(memory_values, swapped), 1), shift_x(after(memory_keys, q1), -1)
    q2 = shift_z(after(q_pack, q3), 2)
    near = flip_tensor(after(swapped, q2), 2)
    q_all = [q_pack, q1, q2, q3]
    stored = jnp.stack([q[rows, 0:16] for q in q_all]).reshape(-1).astype(jnp.int32)

    local_out = pl.pallas_call(
        local_kernel,
        out_shape=jax.ShapeDtypeStruct((rows, width), jnp.float32),
        in_specs=[SM] + [VM] * 4,
        out_specs=VM,
        compiler_params=params,
        cost_estimate=cost(4 * heads * rows * rows * HEAD, heads * rows * rows, 6 * rows * width),
        name="local_attention",
    )(gate, segments.reshape(1, rows), queries, local_keys, local_values)

    parts = pl.pallas_call(
        memory_kernel,
        out_shape=jax.ShapeDtypeStruct((NZ, rows + EXTRA, width), jnp.bfloat16),
        in_specs=[SM] * 2 + [HB] * 12,
        out_specs=VM,
        scratch_shapes=[
            pltpu.VMEM((NZ, rows + EXTRA, width), jnp.bfloat16),
            pltpu.VMEM((NX, SLOTS * BLOCK, width), jnp.bfloat16),
            pltpu.VMEM((NX, SLOTS * BLOCK, width), jnp.bfloat16),
            pltpu.SMEM((2 * NZ * NX + 1,), jnp.int32),
            pltpu.SemaphoreType.DMA((12,)),
        ],
        compiler_params=params,
        cost_estimate=cost(
            64 * heads * rows * rows * HEAD, 8 * heads * rows * rows, 24 * rows * width
        ),
        name="memory_attention",
    )(ids, stored, *in_hbm([*q_all, memory_keys, k1, k2, k3, memory_values, v1, v2, v3]))

    tall = jnp.concatenate([swapped, near], axis=0)
    parts, tall = together(parts, tall)
    back = exchange_z(parts)
    t1, t2, t3 = [shift_y(tall, k) for k in (1, 2, 3)]
    c0 = flip_tensor(tall, 1)
    back, c0, t1, t3 = together(back, c0, t1, t3)
    attention, att_t = pl.pallas_call(
        merge_kernel,
        out_shape=[
            jax.ShapeDtypeStruct((rows, width), jnp.bfloat16),
            jax.ShapeDtypeStruct((NZ, width, rows), jnp.bfloat16),
        ],
        in_specs=[SM] + [VM] * 2,
        out_specs=[VM] * 2,
        compiler_params=params,
        cost_estimate=cost(32 * rows * width, 4 * rows, 16 * rows * width),
        name="merge",
    )(gate, local_out, back)
    att_t, t1, t2, t3 = together(att_t, t1, t2, t3)
    att_all = exchange_z(att_t)
    tall = in_hbm([tall, t1, t2, t3, c0] + [flip_tensor(v, 1) for v in (t1, t2, t3)])
    grads = pl.pallas_call(
        grad_kernel,
        out_shape=jax.ShapeDtypeStruct((NZ, rows, width), jnp.bfloat16),
        in_specs=[SM] + [HB] * 9,
        out_specs=VM,
        scratch_shapes=[
            pltpu.VMEM((NY, rows, 4 * width), jnp.bfloat16),
            pltpu.VMEM((width, 4 * width), jnp.bfloat16),
            pltpu.SemaphoreType.DMA((20,)),
        ],
        compiler_params=params,
        cost_estimate=cost(32 * rows * width * width, 0, 48 * rows * width),
        name="attention_grad",
    )(ids, *tall, *in_hbm([out_weight]))
    att_all, grads = together(att_all, grads)

    mine, *sent = pl.pallas_call(
        weight_kernel,
        out_shape=[jax.ShapeDtypeStruct((width, width), jnp.float32)]
        + [jax.ShapeDtypeStruct((width, width), jnp.bfloat16)] * 3,
        in_specs=[SM, VM] + [HB] * 8,
        out_specs=[VM] * 4,
        scratch_shapes=[
            pltpu.VMEM((width, NZ * rows), jnp.bfloat16),
            pltpu.VMEM((4, NY * rows, width), jnp.bfloat16),
            pltpu.SemaphoreType.DMA((16,)),
        ],
        compiler_params=params,
        cost_estimate=cost(32 * rows * width * width, 0, 48 * rows * width),
        name="weight_partials",
    )(ids, att_all, *tall)
    got = [shift_x(sent[n - 1], n) for n in (1, 2, 3)]
    attention_grad = jnp.sum(exchange_z(after(grads, mine)).astype(jnp.float32), axis=0).astype(jnp.bfloat16)
    weight_grad = (mine + got[0].astype(jnp.float32)) + (
        got[1].astype(jnp.float32) + got[2].astype(jnp.float32)
    )
    return (attention, attention_grad, weight_grad)


def solution(mesh):
    return jax.shard_map(
        per_device,
        mesh=mesh,
        in_specs=(
            P("mem", "tensor"),
            P("mem", "tensor"),
            P("mem", "tensor"),
            P("mem"),
            P("mem", "tensor"),
            P("mem", "tensor"),
            P("mem", None),
            P(),
            P("tensor"),
            P("tensor", None),
            P("mem", "tensor"),
        ),
        out_specs=(P("mem", "tensor"), P("mem", "tensor"), P("tensor", "mem")),
        check_vma=False,
    )
```

```python
import jax
import jax.numpy as jnp
from jax import lax
from jax.experimental import pallas as pl
from jax.experimental.pallas import tpu as pltpu
from jax.sharding import PartitionSpec as P

HEAD = 128
BLOCK = 128
SLOTS = 4
NX = 4
NZ = 4
NY = 4
LOG2E = 1.4426950408889634
SCALE2 = HEAD**-0.5 * LOG2E
NEG = -1e30
EXTRA = 16

VM = pl.BlockSpec(memory_space=pltpu.VMEM)
SM = pl.BlockSpec(memory_space=pltpu.SMEM)
HB = pl.BlockSpec(memory_space=pltpu.HBM)


def cost(flops, transcendentals, bytes_accessed):
    return pl.CostEstimate(
        flops=flops, transcendentals=transcendentals, bytes_accessed=bytes_accessed
    )


def in_hbm(values):
    return [pltpu.with_memory_space_constraint(v, pltpu.HBM) for v in values]


def together(*values):
    return lax.optimization_barrier(values)


def after(value, *deps):
    return lax.optimization_barrier((value, *deps))[0]


def dot_nt(a, b):
    return lax.dot_general(a, b, (((1,), (1,)), ((), ())), preferred_element_type=jnp.float32)


def dot_nn(a, b):
    return lax.dot_general(a, b, (((1,), (0,)), ((), ())), preferred_element_type=jnp.float32)


def shift_x(value, k):
    pairs = [(z * NX + x, z * NX + (x + k) % NX) for z in range(NZ) for x in range(NX)]
    return lax.ppermute(value, "mem", pairs)


def shift_z(value, k):
    pairs = [(z * NX + x, (z + k) % NZ * NX + x) for z in range(NZ) for x in range(NX)]
    return lax.ppermute(value, "mem", pairs)


def exchange_z(value):
    groups = [[z * NX + x for z in range(NZ)] for x in range(NX)]
    return lax.all_to_all(
        value, "mem", split_axis=0, concat_axis=0, axis_index_groups=groups, tiled=True
    )


def shift_y(value, k):
    pairs = [(y * 4 + r, (y + k) % NY * 4 + r) for y in range(NY) for r in range(4)]
    return lax.ppermute(value, "tensor", pairs)


def gather_y(value):
    return [value] + [shift_y(value, k) for k in (1, 2, 3)]


def flip_tensor(value, bit):
    return lax.ppermute(value, "tensor", [(t, t ^ bit) for t in range(16)])


def stored_in(*packs):
    rows = packs[0].shape[0] - EXTRA
    return jnp.concatenate([q[rows, 0:16] for q in packs]).astype(jnp.int32)


def move_zy(value, target):
    pairs = []
    for z in range(NZ):
        for y in range(NY):
            to_z, to_y = target(z, y)
            for x in range(NX):
                for r in range(4):
                    source = (z * NX + x) * 16 + y * 4 + r
                    pairs.append((source, (to_z * NX + x) * 16 + to_y * 4 + r))
    return lax.ppermute(value, ("mem", "tensor"), pairs)


def local_kernel(gate_ref, seg_ref, q_ref, k_ref, v_ref, out_ref):
    rows = q_ref.shape[0]
    heads = q_ref.shape[1] // HEAD
    seg_cols = jnp.broadcast_to(seg_ref[...].astype(jnp.float32), (rows, rows))
    seg_rows = seg_cols.T
    row_ids = lax.broadcasted_iota(jnp.int32, (rows, rows), 0)
    col_ids = lax.broadcasted_iota(jnp.int32, (rows, rows), 1)
    allowed = (col_ids <= row_ids) & (seg_cols == seg_rows)
    for h in range(heads):
        cols = pl.ds(h * HEAD, HEAD)
        scores = jnp.where(allowed, dot_nt(q_ref[:, cols], k_ref[:, cols]) * SCALE2, NEG)
        top = jnp.max(scores, axis=1, keepdims=True)
        weights = jnp.exp2(scores - top)
        total = jnp.sum(weights, axis=1, keepdims=True)
        out = dot_nn(weights.astype(jnp.bfloat16), v_ref[:, cols])
        out_ref[:, cols] = out * ((1.0 - gate_ref[h]) / total)


def memory_kernel(ids_ref, early_ref, late_ref, *refs):
    sources, result_ref = refs[0:12], refs[12]
    q_buf, k_buf, v_buf, sel_ref, sems = refs[13:18]
    targets = [buf.at[n] for buf in (q_buf, k_buf, v_buf) for n in range(4)]
    copies = [
        pltpu.make_async_copy(src, dst, sems.at[n])
        for n, (src, dst) in enumerate(zip(sources, targets))
    ]
    for copy in copies:
        copy.start()

    z, x = ids_ref[0], ids_ref[1]
    for n in range(2 * NZ * NX):
        sel_ref[n] = -1
    for n in range(2 * NZ * 8):
        j = n // 16
        block = late_ref[n % 16] if j == 2 else early_ref[min(j, 2) * 16 + n % 16]
        shard = block // SLOTS
        place = n // 8 * NX + ((x - shard) & 3)
        sel_ref[jnp.where(shard // NX == z, place, 2 * NZ * NX)] = block % SLOTS

    for copy in copies[0:8]:
        copy.wait()
    q_refs, k_refs, v_refs = [[buf.at[n] for n in range(4)] for buf in (q_buf, k_buf, v_buf)]
    heads = k_buf.shape[2] // HEAD
    lane = lax.broadcasted_iota(jnp.int32, (BLOCK, BLOCK), 1)
    for j in range(NZ):
        q_ref, out_ref = q_refs[j], result_ref.at[(z - j) & 3]

        for b in range(2):
            row = b * BLOCK
            stat = jnp.zeros((BLOCK, BLOCK), jnp.float32)
            starts, biases = [], []
            for i in range(NX):
                slot = sel_ref[(2 * j + b) * NX + i]
                starts.append(pl.multiple_of(jnp.maximum(slot, 0) * BLOCK, BLOCK))
                biases.append(
                    jnp.full((1, BLOCK), jnp.where(slot >= 0, 0.0, NEG), jnp.float32)
                )
            bias = jnp.concatenate(biases, axis=1)
            for h in range(heads):
                cols = pl.ds(h * HEAD, HEAD)
                query = q_ref[pl.ds(row, BLOCK), cols]
                keys = jnp.concatenate([k_refs[i][pl.ds(starts[i], BLOCK), cols] for i in range(NX)])
                scores = dot_nt(query, keys) * SCALE2 + bias
                top = jnp.max(scores, axis=1, keepdims=True)
                weights = jnp.exp2(scores - top)
                total = jnp.sum(weights, axis=1, keepdims=True)
                if (j, b, h) == (0, 0, 0):
                    for copy in copies[8:12]:
                        copy.wait()
                values = jnp.concatenate(
                    [v_refs[i][pl.ds(starts[i], BLOCK), cols] for i in range(NX)]
                )
                acc = dot_nn(weights.astype(jnp.bfloat16), values)
                out_ref[pl.ds(row, BLOCK), cols] = (acc / total).astype(jnp.bfloat16)
                stat = jnp.where(lane == h, top + jnp.log2(total), stat)
            stat = stat.T[0:8]
            high = stat.astype(jnp.bfloat16)
            rest = stat - high.astype(jnp.float32)
            mid = rest.astype(jnp.bfloat16)
            low = rest - mid.astype(jnp.float32)
            packed = jnp.concatenate(
                [
                    high[0:4].astype(jnp.float32),
                    mid[0:4].astype(jnp.float32),
                    low[0:4],
                    jnp.zeros((4, BLOCK), jnp.float32),
                ],
                axis=0,
            )
            out_ref[2 * BLOCK : 2 * BLOCK + EXTRA, pl.ds(row, BLOCK)] = packed.astype(jnp.bfloat16)
        out_ref[2 * BLOCK : 2 * BLOCK + EXTRA, 2 * BLOCK :] = jnp.zeros(
            (EXTRA, out_ref.shape[1] - 2 * BLOCK), jnp.bfloat16
        )


def merge_kernel(gate_ref, local_ref, back_ref, att_ref, att_t_ref):
    parts = [back_ref.at[n] for n in range(NZ)]
    heads = local_ref.shape[1] // HEAD
    for b in range(2):
        rows = pl.ds(b * BLOCK, BLOCK)
        logs = []
        for p in parts:
            s = p[2 * BLOCK : 2 * BLOCK + EXTRA, rows].astype(jnp.float32)
            logs.append((s[0:4] + s[4:8]) + s[8:12])
        top = jnp.maximum(jnp.maximum(logs[0], logs[1]), jnp.maximum(logs[2], logs[3]))
        shares = [jnp.exp2(s - top) for s in logs]
        total = (shares[0] + shares[1]) + (shares[2] + shares[3])
        shares = [s / total for s in shares]
        table = jnp.concatenate(shares + [jnp.zeros((BLOCK - 16, BLOCK), jnp.float32)], axis=0).T
        for h in range(heads):
            cols = pl.ds(h * HEAD, HEAD)
            acc = None
            for n, p in enumerate(parts):
                term = p[rows, cols].astype(jnp.float32) * table[:, 4 * n + h : 4 * n + h + 1]
                acc = term if acc is None else acc + term
            out = gate_ref[h] * acc + local_ref[rows, cols]
            att_ref[rows, cols] = out.astype(jnp.bfloat16)
            flipped = out.T.astype(jnp.bfloat16)
            for n in range(NZ):
                att_t_ref[n, cols, rows] = flipped


def grad_kernel(ids_ref, *refs):
    own, other, w_ref, out_ref, acc_ref = refs[0:4], refs[4:8], refs[8], refs[9], refs[10]
    step = pl.program_id(0)
    zl, c = ids_ref[4], ids_ref[5]
    width = own[0].shape[1]
    rows = out_ref.shape[0]

    @pl.when(step == 0)
    def _():
        acc_ref[...] = jnp.zeros_like(acc_ref)

    for k in range(NY):

        @pl.when(step == k)
        def _(k=k):
            acc = acc_ref[...]
            for w, arrays in enumerate((own, other)):
                for s in range(2):
                    place = (zl ^ s) * 2 + (c ^ w)
                    cols = pl.ds(pl.multiple_of(place * width, 128), width)
                    acc = acc + dot_nt(arrays[k][s * rows : (s + 1) * rows, :], w_ref[:, cols])
            acc_ref[...] = acc

    @pl.when(step == NY - 1)
    def _():
        out_ref[...] = acc_ref[...].astype(jnp.bfloat16)


def weight_kernel(ids_ref, *refs):
    att_ref, own, other = refs[0], refs[1:5], refs[5:9]
    outs, att_scr, cot_buf, sems = refs[9:13], refs[13], refs[14], refs[15]
    z, x, y, zl, c = ids_ref[0], ids_ref[1], ids_ref[2], ids_ref[4], ids_ref[5]
    rows = att_ref.shape[2]
    copies = []
    for w, arrays in enumerate((own, other)):
        for s in range(2):
            for k in range(NY):
                n = (2 * w + s) * NY + k
                copies.append(
                    pltpu.make_async_copy(
                        arrays[k].at[pl.ds(s * rows, rows)],
                        cot_buf.at[2 * w + s, pl.ds(k * rows, rows)],
                        sems.at[n],
                    )
                )
                copies[-1].start()
    for j in range(NZ):
        place = ((y - z - j) & 3) * rows
        att_scr[:, pl.ds(pl.multiple_of(place, 128), rows)] = att_ref[j]
    for w in range(2):
        for s in range(2):
            for copy in copies[(2 * w + s) * NY : (2 * w + s + 1) * NY]:
                copy.wait()
            acc = dot_nn(att_scr[...], cot_buf[2 * w + s])
            target = (((zl ^ s) * 2 + (c ^ w)) - x) & 3

            for n in range(NX):

                @pl.when(target == n)
                def _(n=n, acc=acc):
                    outs[n][...] = acc.astype(outs[n].dtype)


def per_device(
    queries,
    local_keys,
    local_values,
    segments,
    memory_keys,
    memory_values,
    retrieved,
    block_slot,
    gate_bias,
    out_weight,
    cotangent,
):
    rows, width = queries.shape
    heads = width // HEAD
    mem, ten = lax.axis_index("mem"), lax.axis_index("tensor")
    z, x = mem // NX, mem % NX
    y, zl, c = ten // 4, (ten // 2) % 2, ten % 2
    ids = jnp.stack([z, x, y, jnp.zeros_like(z), zl, c]).astype(jnp.int32)
    gate = jax.nn.sigmoid(gate_bias)
    params = pltpu.CompilerParams(vmem_limit_bytes=16 << 20)

    names = jnp.arange(block_slot.shape[0], dtype=jnp.int32)
    storage = jnp.sum(
        jnp.where(retrieved.reshape(-1)[:, None] == names[None, :], block_slot[None, :], 0), axis=1
    )
    extra = jnp.zeros((EXTRA, width), jnp.bfloat16)
    extra = extra.at[0, 0 : storage.shape[0]].set(storage.astype(jnp.bfloat16))
    q_pack = jnp.concatenate([queries, extra], axis=0)

    k1, v3, q1, q3, moved, own_keys, own_values, own_cot, q_pack = together(
        shift_x(memory_keys, 1),
        shift_x(memory_values, -1),
        shift_z(q_pack, 1),
        shift_z(q_pack, 3),
        move_zy(cotangent, lambda z, y: (z, (y + z) % NY)),
        memory_keys,
        memory_values,
        cotangent,
        q_pack,
    )
    k2, v2, v1, q2 = shift_x(k1, 1), shift_x(v3, -1), shift_x(own_values, 1), shift_z(q_pack, 2)
    swapped = move_zy(moved, lambda z, y: ((y - z) % NZ, y))
    k3 = shift_x(after(own_keys, v2), -1)
    early = stored_in(q_pack, q1, q3)
    k2, v1, q2, k3, swapped, own_cot, early = together(k2, v1, q2, k3, swapped, own_cot, early)
    near, near_own = flip_tensor(swapped, 2), flip_tensor(own_cot, 2)
    q_all = [q_pack, q1, q2, q3]

    local_out = pl.pallas_call(
        local_kernel,
        out_shape=jax.ShapeDtypeStruct((rows, width), jnp.float32),
        in_specs=[SM] + [VM] * 4,
        out_specs=VM,
        compiler_params=params,
        cost_estimate=cost(4 * heads * rows * rows * HEAD, heads * rows * rows, 6 * rows * width),
        name="local_attention",
    )(gate, segments.reshape(1, rows), queries, local_keys, local_values)

    parts = pl.pallas_call(
        memory_kernel,
        out_shape=jax.ShapeDtypeStruct((NZ, rows + EXTRA, width), jnp.bfloat16),
        in_specs=[SM] * 3 + [HB] * 12,
        out_specs=VM,
        scratch_shapes=[
            pltpu.VMEM((NZ, rows + EXTRA, width), jnp.bfloat16),
            pltpu.VMEM((NX, SLOTS * BLOCK, width), jnp.bfloat16),
            pltpu.VMEM((NX, SLOTS * BLOCK, width), jnp.bfloat16),
            pltpu.SMEM((2 * NZ * NX + 1,), jnp.int32),
            pltpu.SemaphoreType.DMA((12,)),
        ],
        compiler_params=params,
        cost_estimate=cost(
            64 * heads * rows * rows * HEAD, 8 * heads * rows * rows, 24 * rows * width
        ),
        name="memory_attention",
    )(ids, early, stored_in(q2), *in_hbm([*q_all, memory_keys, k1, k2, k3, memory_values, v1, v2, v3]))

    tall = jnp.concatenate([swapped, near], axis=0)
    wide = jnp.concatenate([cotangent, near_own], axis=0)
    parts, tall, wide = together(parts, tall, wide)
    back = exchange_z(parts)
    t1, t2, t3 = [shift_y(tall, k) for k in (1, 2, 3)]
    c0 = flip_tensor(tall, 1)
    back, c0, t1, t3 = together(back, c0, t1, t3)
    attention, att_t = pl.pallas_call(
        merge_kernel,
        out_shape=[
            jax.ShapeDtypeStruct((rows, width), jnp.bfloat16),
            jax.ShapeDtypeStruct((NZ, width, rows), jnp.bfloat16),
        ],
        in_specs=[SM] + [VM] * 2,
        out_specs=[VM] * 2,
        compiler_params=params,
        cost_estimate=cost(32 * rows * width, 4 * rows, 16 * rows * width),
        name="merge",
    )(gate, local_out, back)
    att_t, t1, t2, t3, wide = together(att_t, t1, t2, t3, wide)
    att_all = exchange_z(att_t)
    tall = in_hbm([tall, t1, t2, t3, c0] + [flip_tensor(v, 1) for v in (t1, t2, t3)])
    w1, w2, w3 = [shift_y(wide, k) for k in (1, 2, 3)]
    wide = [wide, w1, w2, w3] + [flip_tensor(v, 1) for v in (wide, w1, w2, w3)]

    mine, *sent = pl.pallas_call(
        weight_kernel,
        out_shape=[jax.ShapeDtypeStruct((width, width), jnp.float32)]
        + [jax.ShapeDtypeStruct((width, width), jnp.bfloat16)] * 3,
        in_specs=[SM, VM] + [HB] * 8,
        out_specs=[VM] * 4,
        scratch_shapes=[
            pltpu.VMEM((width, NZ * rows), jnp.bfloat16),
            pltpu.VMEM((4, NY * rows, width), jnp.bfloat16),
            pltpu.SemaphoreType.DMA((16,)),
        ],
        compiler_params=params,
        cost_estimate=cost(32 * rows * width * width, 0, 48 * rows * width),
        name="weight_partials",
    )(ids, att_all, *tall)
    got = [shift_x(sent[n - 1], n) for n in (1, 2, 3)]
    attention_grad = pl.pallas_call(
        grad_kernel,
        out_shape=jax.ShapeDtypeStruct((rows, width), jnp.bfloat16),
        grid_spec=pltpu.PrefetchScalarGridSpec(
            num_scalar_prefetch=1,
            grid=(NY,),
            in_specs=[
                pl.BlockSpec(
                    (2 * rows, width), lambda g, ids: (0, 0), pipeline_mode=pl.Buffered(1)
                )
            ]
            * 8
            + [pl.BlockSpec((width, 4 * width), lambda g, ids: (0, (ids[2] - g) & 3))],
            out_specs=pl.BlockSpec((rows, width), lambda g, ids: (0, 0)),
            scratch_shapes=[pltpu.VMEM((rows, width), jnp.float32)],
        ),
        compiler_params=params,
        cost_estimate=cost(32 * rows * width * width, 0, 64 * rows * width),
        name="attention_grad",
    )(after(ids, mine), *wide, *in_hbm([out_weight]))

    weight_grad = (mine + got[0].astype(jnp.float32)) + (
        got[1].astype(jnp.float32) + got[2].astype(jnp.float32)
    )
    return (attention, attention_grad, weight_grad)


def solution(mesh):
    return jax.shard_map(
        per_device,
        mesh=mesh,
        in_specs=(
            P("mem", "tensor"),
            P("mem", "tensor"),
            P("mem", "tensor"),
            P("mem"),
            P("mem", "tensor"),
            P("mem", "tensor"),
            P("mem", None),
            P(),
            P("tensor"),
            P("tensor", None),
            P("mem", "tensor"),
        ),
        out_specs=(P("mem", "tensor"), P("mem", "tensor"), P("tensor", "mem")),
        check_vma=False,
    )
```

```python
import jax
import jax.numpy as jnp
from jax import lax
from jax.experimental import pallas as pl
from jax.experimental.pallas import tpu as pltpu
from jax.sharding import PartitionSpec as P

HEAD = 128
BLOCK = 128
SLOTS = 4
NX = 4
NZ = 4
NY = 4
LOG2E = 1.4426950408889634
SCALE2 = HEAD**-0.5 * LOG2E
NEG = -1e30
EXTRA = 16

VM = pl.BlockSpec(memory_space=pltpu.VMEM)
SM = pl.BlockSpec(memory_space=pltpu.SMEM)
HB = pl.BlockSpec(memory_space=pltpu.HBM)


def cost(flops, transcendentals, bytes_accessed):
    return pl.CostEstimate(
        flops=flops, transcendentals=transcendentals, bytes_accessed=bytes_accessed
    )


def in_hbm(values):
    return [pltpu.with_memory_space_constraint(v, pltpu.HBM) for v in values]


def together(*values):
    return lax.optimization_barrier(values)


def after(value, *deps):
    return lax.optimization_barrier((value, *deps))[0]


def dot_nt(a, b):
    return lax.dot_general(a, b, (((1,), (1,)), ((), ())), preferred_element_type=jnp.float32)


def dot_nn(a, b):
    return lax.dot_general(a, b, (((1,), (0,)), ((), ())), preferred_element_type=jnp.float32)


def shift_x(value, k):
    pairs = [(z * NX + x, z * NX + (x + k) % NX) for z in range(NZ) for x in range(NX)]
    return lax.ppermute(value, "mem", pairs)


def shift_z(value, k):
    pairs = [(z * NX + x, (z + k) % NZ * NX + x) for z in range(NZ) for x in range(NX)]
    return lax.ppermute(value, "mem", pairs)


def exchange_z(value):
    groups = [[z * NX + x for z in range(NZ)] for x in range(NX)]
    return lax.all_to_all(
        value, "mem", split_axis=0, concat_axis=0, axis_index_groups=groups, tiled=True
    )


def shift_y(value, k):
    pairs = [(y * 4 + r, (y + k) % NY * 4 + r) for y in range(NY) for r in range(4)]
    return lax.ppermute(value, "tensor", pairs)


def gather_y(value):
    return [value] + [shift_y(value, k) for k in (1, 2, 3)]


def flip_tensor(value, bit):
    return lax.ppermute(value, "tensor", [(t, t ^ bit) for t in range(16)])


def stored_in(*packs):
    rows = packs[0].shape[0] - EXTRA
    return jnp.concatenate([q[rows, 0:16] for q in packs]).astype(jnp.int32)


def move_zy(value, target):
    pairs = []
    for z in range(NZ):
        for y in range(NY):
            to_z, to_y = target(z, y)
            for x in range(NX):
                for r in range(4):
                    source = (z * NX + x) * 16 + y * 4 + r
                    pairs.append((source, (to_z * NX + x) * 16 + to_y * 4 + r))
    return lax.ppermute(value, ("mem", "tensor"), pairs)


def local_kernel(gate_ref, seg_ref, q_ref, k_ref, v_ref, out_ref):
    rows = q_ref.shape[0]
    heads = q_ref.shape[1] // HEAD
    seg_cols = jnp.broadcast_to(seg_ref[...].astype(jnp.float32), (rows, rows))
    seg_rows = seg_cols.T
    row_ids = lax.broadcasted_iota(jnp.int32, (rows, rows), 0)
    col_ids = lax.broadcasted_iota(jnp.int32, (rows, rows), 1)
    allowed = (col_ids <= row_ids) & (seg_cols == seg_rows)
    for h in range(heads):
        cols = pl.ds(h * HEAD, HEAD)
        scores = jnp.where(allowed, dot_nt(q_ref[:, cols], k_ref[:, cols]) * SCALE2, NEG)
        top = jnp.max(scores, axis=1, keepdims=True)
        weights = jnp.exp2(scores - top)
        total = jnp.sum(weights, axis=1, keepdims=True)
        out = dot_nn(weights.astype(jnp.bfloat16), v_ref[:, cols])
        out_ref[:, cols] = out * ((1.0 - gate_ref[h]) / total)


def memory_kernel(ids_ref, early_ref, late_ref, *refs):
    sources, result_ref = refs[0:12], refs[12]
    q_buf, k_buf, v_buf, sel_ref, sems = refs[13:18]
    targets = [buf.at[n] for buf in (q_buf, k_buf, v_buf) for n in range(4)]
    heads = k_buf.shape[2] // HEAD
    copies = []
    for h in range(heads):
        cols = pl.ds(h * HEAD, HEAD)
        copies.append(
            [
                pltpu.make_async_copy(src.at[:, cols], dst.at[:, cols], sems.at[12 * h + n])
                for n, (src, dst) in enumerate(zip(sources, targets))
            ]
        )
        for copy in copies[h]:
            copy.start()

    z, x = ids_ref[0], ids_ref[1]
    for n in range(2 * NZ * NX):
        sel_ref[n] = -1
    for n in range(2 * NZ * 8):
        j = n // 16
        block = late_ref[n % 16] if j == 2 else early_ref[min(j, 2) * 16 + n % 16]
        shard = block // SLOTS
        place = n // 8 * NX + ((x - shard) & 3)
        sel_ref[jnp.where(shard // NX == z, place, 2 * NZ * NX)] = block % SLOTS

    sub = lax.broadcasted_iota(jnp.int32, (8, BLOCK), 0)
    stats = [jnp.zeros((8, BLOCK), jnp.float32) for _ in range(2 * NZ)]
    for h in range(heads):
        cols = pl.ds(h * HEAD, HEAD)
        for copy in copies[h]:
            copy.wait()
        for n in range(2 * NZ):
            j, b = n // 2, n % 2
            rows = pl.ds(b * BLOCK, BLOCK)
            slots = [sel_ref[n * NX + i] for i in range(NX)]
            places = [
                pl.ds(pl.multiple_of(jnp.maximum(slot, 0) * BLOCK, BLOCK), BLOCK) for slot in slots
            ]
            keys = jnp.concatenate([k_buf[i, places[i], cols] for i in range(NX)])
            values = jnp.concatenate([v_buf[i, places[i], cols] for i in range(NX)])
            products = dot_nt(keys, q_buf[j, rows, cols])
            scores = [
                products[i * BLOCK : (i + 1) * BLOCK] * SCALE2 + jnp.where(slots[i] >= 0, 0.0, NEG)
                for i in range(NX)
            ]
            peak = jnp.maximum(jnp.maximum(scores[0], scores[1]), jnp.maximum(scores[2], scores[3]))
            top = jnp.max(peak, axis=0, keepdims=True)
            weights = [jnp.exp2(s - top) for s in scores]
            total = jnp.sum(
                (weights[0] + weights[1]) + (weights[2] + weights[3]), axis=0, keepdims=True
            )
            inverse = 1.0 / total
            weights = jnp.concatenate([(w * inverse).astype(jnp.bfloat16) for w in weights])
            out = lax.dot_general(
                weights, values, (((0,), (0,)), ((), ())), preferred_element_type=jnp.float32
            )
            result_ref[(z - j) & 3, rows, cols] = out.astype(jnp.bfloat16)
            stats[n] = jnp.where(sub == h, top + jnp.log2(total), stats[n])
    for n in range(2 * NZ):
        stat = stats[n]
        high = stat.astype(jnp.bfloat16).astype(jnp.float32)
        mid = (stat - high).astype(jnp.bfloat16).astype(jnp.float32)
        low = (stat - high) - mid
        packed = jnp.concatenate(
            [high[0:4], mid[0:4], low[0:4], jnp.zeros((4, BLOCK), jnp.float32)], axis=0
        )
        target = result_ref.at[(z - n // 2) & 3]
        target[2 * BLOCK : 2 * BLOCK + EXTRA, pl.ds(n % 2 * BLOCK, BLOCK)] = packed.astype(
            jnp.bfloat16
        )
    for j in range(NZ):
        result_ref[j, 2 * BLOCK : 2 * BLOCK + EXTRA, 2 * BLOCK :] = jnp.zeros(
            (EXTRA, result_ref.shape[2] - 2 * BLOCK), jnp.bfloat16
        )


def merge_kernel(gate_ref, local_ref, back_ref, att_ref, att_t_ref):
    parts = [back_ref.at[n] for n in range(NZ)]
    heads = local_ref.shape[1] // HEAD
    for b in range(2):
        rows = pl.ds(b * BLOCK, BLOCK)
        logs = []
        for p in parts:
            s = p[2 * BLOCK : 2 * BLOCK + EXTRA, rows].astype(jnp.float32)
            logs.append((s[0:4] + s[4:8]) + s[8:12])
        top = jnp.maximum(jnp.maximum(logs[0], logs[1]), jnp.maximum(logs[2], logs[3]))
        shares = [jnp.exp2(s - top) for s in logs]
        total = (shares[0] + shares[1]) + (shares[2] + shares[3])
        shares = [s / total for s in shares]
        table = jnp.concatenate(shares + [jnp.zeros((BLOCK - 16, BLOCK), jnp.float32)], axis=0).T
        for h in range(heads):
            cols = pl.ds(h * HEAD, HEAD)
            acc = None
            for n, p in enumerate(parts):
                term = p[rows, cols].astype(jnp.float32) * table[:, 4 * n + h : 4 * n + h + 1]
                acc = term if acc is None else acc + term
            out = gate_ref[h] * acc + local_ref[rows, cols]
            att_ref[rows, cols] = out.astype(jnp.bfloat16)
            flipped = out.T.astype(jnp.bfloat16)
            for n in range(NZ):
                att_t_ref[n, cols, rows] = flipped


def grad_kernel(ids_ref, *refs):
    own, other, w_ref, out_ref, acc_ref = refs[0:4], refs[4:8], refs[8], refs[9], refs[10]
    step = pl.program_id(0)
    zl, c = ids_ref[4], ids_ref[5]
    width = own[0].shape[1]
    rows = out_ref.shape[0]

    @pl.when(step == 0)
    def _():
        acc_ref[...] = jnp.zeros_like(acc_ref)

    for k in range(NY):

        @pl.when(step == k)
        def _(k=k):
            acc = acc_ref[...]
            for w, arrays in enumerate((own, other)):
                for s in range(2):
                    place = (zl ^ s) * 2 + (c ^ w)
                    cols = pl.ds(pl.multiple_of(place * width, 128), width)
                    acc = acc + dot_nt(arrays[k][s * rows : (s + 1) * rows, :], w_ref[:, cols])
            acc_ref[...] = acc

    @pl.when(step == NY - 1)
    def _():
        out_ref[...] = acc_ref[...].astype(jnp.bfloat16)


def weight_kernel(ids_ref, *refs):
    att_ref, own, other = refs[0], refs[1:5], refs[5:9]
    outs, att_scr, cot_buf, sems = refs[9:13], refs[13], refs[14], refs[15]
    z, x, y, zl, c = ids_ref[0], ids_ref[1], ids_ref[2], ids_ref[4], ids_ref[5]
    rows = att_ref.shape[2]
    copies = []
    for w, arrays in enumerate((own, other)):
        for s in range(2):
            for k in range(NY):
                n = (2 * w + s) * NY + k
                copies.append(
                    pltpu.make_async_copy(
                        arrays[k].at[pl.ds(s * rows, rows)],
                        cot_buf.at[2 * w + s, pl.ds(k * rows, rows)],
                        sems.at[n],
                    )
                )
                copies[-1].start()
    for j in range(NZ):
        place = ((y - z - j) & 3) * rows
        att_scr[:, pl.ds(pl.multiple_of(place, 128), rows)] = att_ref[j]
    for w in range(2):
        for s in range(2):
            for copy in copies[(2 * w + s) * NY : (2 * w + s + 1) * NY]:
                copy.wait()
            acc = dot_nn(att_scr[...], cot_buf[2 * w + s])
            target = (((zl ^ s) * 2 + (c ^ w)) - x) & 3

            for n in range(NX):

                @pl.when(target == n)
                def _(n=n, acc=acc):
                    outs[n][...] = acc.astype(outs[n].dtype)


def per_device(
    queries,
    local_keys,
    local_values,
    segments,
    memory_keys,
    memory_values,
    retrieved,
    block_slot,
    gate_bias,
    out_weight,
    cotangent,
):
    rows, width = queries.shape
    heads = width // HEAD
    mem, ten = lax.axis_index("mem"), lax.axis_index("tensor")
    z, x = mem // NX, mem % NX
    y, zl, c = ten // 4, (ten // 2) % 2, ten % 2
    ids = jnp.stack([z, x, y, jnp.zeros_like(z), zl, c]).astype(jnp.int32)
    gate = jax.nn.sigmoid(gate_bias)
    params = pltpu.CompilerParams(vmem_limit_bytes=16 << 20)

    names = jnp.arange(block_slot.shape[0], dtype=jnp.int32)
    storage = jnp.sum(
        jnp.where(retrieved.reshape(-1)[:, None] == names[None, :], block_slot[None, :], 0), axis=1
    )
    extra = jnp.zeros((EXTRA, width), jnp.bfloat16)
    extra = extra.at[0, 0 : storage.shape[0]].set(storage.astype(jnp.bfloat16))
    q_pack = jnp.concatenate([queries, extra], axis=0)

    k1, v3, q1, q3, moved, own_keys, own_values, own_cot, q_pack = together(
        shift_x(memory_keys, 1),
        shift_x(memory_values, -1),
        shift_z(q_pack, 1),
        shift_z(q_pack, 3),
        move_zy(cotangent, lambda z, y: (z, (y + z) % NY)),
        memory_keys,
        memory_values,
        cotangent,
        q_pack,
    )
    q2 = shift_z(q_pack, 2)
    swapped = move_zy(moved, lambda z, y: ((y - z) % NZ, y))
    v1, k2, v2 = shift_x(own_values, 1), shift_x(k1, 1), shift_x(v3, -1)
    k3 = shift_x(after(own_keys, v2), -1)
    early = stored_in(q_pack, q1, q3)
    k2, v1, q2, k3, swapped, own_cot, early = together(k2, v1, q2, k3, swapped, own_cot, early)
    near, near_own = flip_tensor(swapped, 2), flip_tensor(own_cot, 2)
    q_all = [q_pack, q1, q2, q3]

    local_out = pl.pallas_call(
        local_kernel,
        out_shape=jax.ShapeDtypeStruct((rows, width), jnp.float32),
        in_specs=[SM] + [VM] * 4,
        out_specs=VM,
        compiler_params=params,
        cost_estimate=cost(4 * heads * rows * rows * HEAD, heads * rows * rows, 6 * rows * width),
        name="local_attention",
    )(gate, segments.reshape(1, rows), queries, local_keys, local_values)

    parts = pl.pallas_call(
        memory_kernel,
        out_shape=jax.ShapeDtypeStruct((NZ, rows + EXTRA, width), jnp.bfloat16),
        in_specs=[SM] * 3 + [HB] * 12,
        out_specs=VM,
        scratch_shapes=[
            pltpu.VMEM((NZ, rows + EXTRA, width), jnp.bfloat16),
            pltpu.VMEM((NX, SLOTS * BLOCK, width), jnp.bfloat16),
            pltpu.VMEM((NX, SLOTS * BLOCK, width), jnp.bfloat16),
            pltpu.SMEM((2 * NZ * NX + 1,), jnp.int32),
            pltpu.SemaphoreType.DMA((12 * heads,)),
        ],
        compiler_params=params,
        cost_estimate=cost(
            64 * heads * rows * rows * HEAD, 8 * heads * rows * rows, 24 * rows * width
        ),
        name="memory_attention",
    )(ids, early, stored_in(q2), *in_hbm([*q_all, memory_keys, k1, k2, k3, memory_values, v1, v2, v3]))

    tall = jnp.concatenate([swapped, near], axis=0)
    wide = jnp.concatenate([cotangent, near_own], axis=0)
    parts, tall, wide = together(parts, tall, wide)
    back = exchange_z(parts)
    t1, t3, w1, w3 = [shift_y(v, k) for v in (tall, wide) for k in (1, 3)]
    back, t1, t3, w1, w3 = together(back, t1, t3, w1, w3)
    attention, att_t = pl.pallas_call(
        merge_kernel,
        out_shape=[
            jax.ShapeDtypeStruct((rows, width), jnp.bfloat16),
            jax.ShapeDtypeStruct((NZ, width, rows), jnp.bfloat16),
        ],
        in_specs=[SM] + [VM] * 2,
        out_specs=[VM] * 2,
        compiler_params=params,
        cost_estimate=cost(32 * rows * width, 4 * rows, 16 * rows * width),
        name="merge",
    )(gate, local_out, back)
    att_t, tall, wide, t1, t3, w1, w3 = together(att_t, tall, wide, t1, t3, w1, w3)
    att_all = exchange_z(att_t)
    tall = [tall, t1, shift_y(tall, 2), t3]
    wide = [wide, w1, shift_y(wide, 2), w3]
    flipped = [flip_tensor(v, 1) for v in tall + [wide[0], wide[1], wide[3]]]
    att_all, *flipped = together(att_all, *flipped)
    tall = in_hbm(tall + flipped[:4])

    mine, *sent = pl.pallas_call(
        weight_kernel,
        out_shape=[jax.ShapeDtypeStruct((width, width), jnp.float32)]
        + [jax.ShapeDtypeStruct((width, width), jnp.bfloat16)] * 3,
        in_specs=[SM, VM] + [HB] * 8,
        out_specs=[VM] * 4,
        scratch_shapes=[
            pltpu.VMEM((width, NZ * rows), jnp.bfloat16),
            pltpu.VMEM((4, NY * rows, width), jnp.bfloat16),
            pltpu.SemaphoreType.DMA((16,)),
        ],
        compiler_params=params,
        cost_estimate=cost(32 * rows * width * width, 0, 48 * rows * width),
        name="weight_partials",
    )(ids, att_all, *tall)
    got = [shift_x(sent[n - 1], n) for n in (1, 3, 2)]
    wide = wide + flipped[4:6] + [flip_tensor(after(wide[2], mine), 1), flipped[6]]
    attention_grad = pl.pallas_call(
        grad_kernel,
        out_shape=jax.ShapeDtypeStruct((rows, width), jnp.bfloat16),
        grid_spec=pltpu.PrefetchScalarGridSpec(
            num_scalar_prefetch=1,
            grid=(NY,),
            in_specs=[
                pl.BlockSpec(
                    (2 * rows, width), lambda g, ids: (0, 0), pipeline_mode=pl.Buffered(1)
                )
            ]
            * 8
            + [pl.BlockSpec((width, 4 * width), lambda g, ids: (0, (ids[2] - g) & 3))],
            out_specs=pl.BlockSpec((rows, width), lambda g, ids: (0, 0)),
            scratch_shapes=[pltpu.VMEM((rows, width), jnp.float32)],
        ),
        compiler_params=params,
        cost_estimate=cost(32 * rows * width * width, 0, 64 * rows * width),
        name="attention_grad",
    )(ids, *wide, *in_hbm([out_weight]))

    attention_grad, *got = together(attention_grad, *got)
    weight_grad = (mine + got[0].astype(jnp.float32)) + (
        got[1].astype(jnp.float32) + got[2].astype(jnp.float32)
    )
    return (attention, attention_grad, weight_grad)


def solution(mesh):
    return jax.shard_map(
        per_device,
        mesh=mesh,
        in_specs=(
            P("mem", "tensor"),
            P("mem", "tensor"),
            P("mem", "tensor"),
            P("mem"),
            P("mem", "tensor"),
            P("mem", "tensor"),
            P("mem", None),
            P(),
            P("tensor"),
            P("tensor", None),
            P("mem", "tensor"),
        ),
        out_specs=(P("mem", "tensor"), P("mem", "tensor"), P("tensor", "mem")),
        check_vma=False,
    )
```

```python
import jax
import jax.numpy as jnp
from jax import lax
from jax.experimental import pallas as pl
from jax.experimental.pallas import tpu as pltpu
from jax.sharding import PartitionSpec as P

HEAD = 128
BLOCK = 128
SLOTS = 4
NX = 4
NZ = 4
NY = 4
LOG2E = 1.4426950408889634
SCALE2 = HEAD**-0.5 * LOG2E
NEG = -1e30
EXTRA = 16

VM = pl.BlockSpec(memory_space=pltpu.VMEM)
SM = pl.BlockSpec(memory_space=pltpu.SMEM)
HB = pl.BlockSpec(memory_space=pltpu.HBM)


def cost(flops, transcendentals, bytes_accessed):
    return pl.CostEstimate(
        flops=flops, transcendentals=transcendentals, bytes_accessed=bytes_accessed
    )


def in_hbm(values):
    return [pltpu.with_memory_space_constraint(v, pltpu.HBM) for v in values]


def together(*values):
    return lax.optimization_barrier(values)


def after(value, *deps):
    return lax.optimization_barrier((value, *deps))[0]


def dot_nt(a, b):
    return lax.dot_general(a, b, (((1,), (1,)), ((), ())), preferred_element_type=jnp.float32)


def dot_nn(a, b):
    return lax.dot_general(a, b, (((1,), (0,)), ((), ())), preferred_element_type=jnp.float32)


def shift_x(value, k):
    pairs = [(z * NX + x, z * NX + (x + k) % NX) for z in range(NZ) for x in range(NX)]
    return lax.ppermute(value, "mem", pairs)


def shift_z(value, k):
    pairs = [(z * NX + x, (z + k) % NZ * NX + x) for z in range(NZ) for x in range(NX)]
    return lax.ppermute(value, "mem", pairs)


def exchange_z(value):
    groups = [[z * NX + x for z in range(NZ)] for x in range(NX)]
    return lax.all_to_all(
        value, "mem", split_axis=0, concat_axis=0, axis_index_groups=groups, tiled=True
    )


def shift_y(value, k):
    pairs = [(y * 4 + r, (y + k) % NY * 4 + r) for y in range(NY) for r in range(4)]
    return lax.ppermute(value, "tensor", pairs)


def gather_y(value):
    return [value] + [shift_y(value, k) for k in (1, 2, 3)]


def flip_tensor(value, bit):
    return lax.ppermute(value, "tensor", [(t, t ^ bit) for t in range(16)])


def stored_in(*packs):
    rows = packs[0].shape[0] - EXTRA
    return jnp.concatenate([q[rows, 0:16] for q in packs]).astype(jnp.int32)


def move_zy(value, target):
    pairs = []
    for z in range(NZ):
        for y in range(NY):
            to_z, to_y = target(z, y)
            for x in range(NX):
                for r in range(4):
                    source = (z * NX + x) * 16 + y * 4 + r
                    pairs.append((source, (to_z * NX + x) * 16 + to_y * 4 + r))
    return lax.ppermute(value, ("mem", "tensor"), pairs)


def local_kernel(gate_ref, seg_ref, q_ref, k_ref, v_ref, out_ref):
    rows = q_ref.shape[0]
    heads = q_ref.shape[1] // HEAD
    seg_cols = jnp.broadcast_to(seg_ref[...].astype(jnp.float32), (rows, rows))
    seg_rows = seg_cols.T
    row_ids = lax.broadcasted_iota(jnp.int32, (rows, rows), 0)
    col_ids = lax.broadcasted_iota(jnp.int32, (rows, rows), 1)
    allowed = (col_ids <= row_ids) & (seg_cols == seg_rows)
    for h in range(heads):
        cols = pl.ds(h * HEAD, HEAD)
        scores = jnp.where(allowed, dot_nt(q_ref[:, cols], k_ref[:, cols]) * SCALE2, NEG)
        top = jnp.max(scores, axis=1, keepdims=True)
        weights = jnp.exp2(scores - top)
        total = jnp.sum(weights, axis=1, keepdims=True)
        out = dot_nn(weights.astype(jnp.bfloat16), v_ref[:, cols])
        out_ref[:, cols] = out * ((1.0 - gate_ref[h]) / total)


def memory_kernel(ids_ref, early_ref, late_ref, *refs):
    sources, result_ref = refs[0:12], refs[12]
    q_buf, k_buf, v_buf, sel_ref, sems = refs[13:18]
    targets = [buf.at[n] for buf in (q_buf, k_buf, v_buf) for n in range(4)]
    heads = k_buf.shape[2] // HEAD
    copies = []
    for h in range(heads):
        cols = pl.ds(h * HEAD, HEAD)
        copies.append(
            [
                pltpu.make_async_copy(src.at[:, cols], dst.at[:, cols], sems.at[12 * h + n])
                for n, (src, dst) in enumerate(zip(sources, targets))
            ]
        )
        for copy in copies[h]:
            copy.start()

    z, x = ids_ref[0], ids_ref[1]
    for n in range(2 * NZ * NX):
        sel_ref[n] = -1
    for n in range(2 * NZ * 8):
        j = n // 16
        block = late_ref[n % 16] if j == 2 else early_ref[min(j, 2) * 16 + n % 16]
        shard = block // SLOTS
        place = n // 8 * NX + ((x - shard) & 3)
        sel_ref[jnp.where(shard // NX == z, place, 2 * NZ * NX)] = block % SLOTS

    sub = lax.broadcasted_iota(jnp.int32, (8, BLOCK), 0)
    stats = [jnp.zeros((8, BLOCK), jnp.float32) for _ in range(2 * NZ)]
    for h in range(heads):
        cols = pl.ds(h * HEAD, HEAD)
        for copy in copies[h]:
            copy.wait()
        for n in range(2 * NZ):
            j, b = n // 2, n % 2
            rows = pl.ds(b * BLOCK, BLOCK)
            slots = [sel_ref[n * NX + i] for i in range(NX)]
            places = [
                pl.ds(pl.multiple_of(jnp.maximum(slot, 0) * BLOCK, BLOCK), BLOCK) for slot in slots
            ]
            keys = jnp.concatenate([k_buf[i, places[i], cols] for i in range(NX)])
            values = jnp.concatenate([v_buf[i, places[i], cols] for i in range(NX)])
            products = dot_nt(keys, q_buf[j, rows, cols])
            scores = [
                products[i * BLOCK : (i + 1) * BLOCK] * SCALE2 + jnp.where(slots[i] >= 0, 0.0, NEG)
                for i in range(NX)
            ]
            peak = jnp.maximum(jnp.maximum(scores[0], scores[1]), jnp.maximum(scores[2], scores[3]))
            top = jnp.max(peak, axis=0, keepdims=True)
            weights = [jnp.exp2(s - top) for s in scores]
            total = jnp.sum(
                (weights[0] + weights[1]) + (weights[2] + weights[3]), axis=0, keepdims=True
            )
            inverse = 1.0 / total
            weights = jnp.concatenate([(w * inverse).astype(jnp.bfloat16) for w in weights])
            out = lax.dot_general(
                weights, values, (((0,), (0,)), ((), ())), preferred_element_type=jnp.float32
            )
            result_ref[(z - j) & 3, rows, cols] = out.astype(jnp.bfloat16)
            stats[n] = jnp.where(sub == h, top + jnp.log2(total), stats[n])
    for n in range(2 * NZ):
        stat = stats[n]
        high = stat.astype(jnp.bfloat16).astype(jnp.float32)
        mid = (stat - high).astype(jnp.bfloat16).astype(jnp.float32)
        low = (stat - high) - mid
        packed = jnp.concatenate(
            [high[0:4], mid[0:4], low[0:4], jnp.zeros((4, BLOCK), jnp.float32)], axis=0
        )
        target = result_ref.at[(z - n // 2) & 3]
        target[2 * BLOCK : 2 * BLOCK + EXTRA, pl.ds(n % 2 * BLOCK, BLOCK)] = packed.astype(
            jnp.bfloat16
        )
    for j in range(NZ):
        result_ref[j, 2 * BLOCK : 2 * BLOCK + EXTRA, 2 * BLOCK :] = jnp.zeros(
            (EXTRA, result_ref.shape[2] - 2 * BLOCK), jnp.bfloat16
        )


def merge_kernel(gate_ref, local_ref, back_ref, att_ref, att_t_ref):
    parts = [back_ref.at[n] for n in range(NZ)]
    heads = local_ref.shape[1] // HEAD
    for b in range(2):
        rows = pl.ds(b * BLOCK, BLOCK)
        logs = []
        for p in parts:
            s = p[2 * BLOCK : 2 * BLOCK + EXTRA, rows].astype(jnp.float32)
            logs.append((s[0:4] + s[4:8]) + s[8:12])
        top = jnp.maximum(jnp.maximum(logs[0], logs[1]), jnp.maximum(logs[2], logs[3]))
        shares = [jnp.exp2(s - top) for s in logs]
        total = (shares[0] + shares[1]) + (shares[2] + shares[3])
        shares = [s / total for s in shares]
        table = jnp.concatenate(shares + [jnp.zeros((BLOCK - 16, BLOCK), jnp.float32)], axis=0).T
        for h in range(heads):
            cols = pl.ds(h * HEAD, HEAD)
            acc = None
            for n, p in enumerate(parts):
                term = p[rows, cols].astype(jnp.float32) * table[:, 4 * n + h : 4 * n + h + 1]
                acc = term if acc is None else acc + term
            out = gate_ref[h] * acc + local_ref[rows, cols]
            att_ref[rows, cols] = out.astype(jnp.bfloat16)
            flipped = out.T.astype(jnp.bfloat16)
            for n in range(NZ):
                att_t_ref[n, cols, rows] = flipped


def grad_kernel(ids_ref, *refs):
    own, other, w_ref, out_ref, acc_ref = refs[0:4], refs[4:8], refs[8], refs[9], refs[10]
    step = pl.program_id(0)
    zl, c = ids_ref[4], ids_ref[5]
    width = own[0].shape[1]
    rows = out_ref.shape[0]

    @pl.when(step == 0)
    def _():
        acc_ref[...] = jnp.zeros_like(acc_ref)

    for k in range(NY):

        @pl.when(step == k)
        def _(k=k):
            acc = acc_ref[...]
            for w, arrays in enumerate((own, other)):
                for s in range(2):
                    place = (zl ^ s) * 2 + (c ^ w)
                    cols = pl.ds(pl.multiple_of(place * width, 128), width)
                    acc = acc + dot_nt(arrays[k][s * rows : (s + 1) * rows, :], w_ref[:, cols])
            acc_ref[...] = acc

    @pl.when(step == NY - 1)
    def _():
        out_ref[...] = acc_ref[...].astype(jnp.bfloat16)


def weight_kernel(ids_ref, *refs):
    att_ref, own, other = refs[0], refs[1:5], refs[5:9]
    outs, att_scr, cot_buf, sems = refs[9:13], refs[13], refs[14], refs[15]
    z, x, y, zl, c = ids_ref[0], ids_ref[1], ids_ref[2], ids_ref[4], ids_ref[5]
    rows = att_ref.shape[2]
    copies = []
    for w, arrays in enumerate((own, other)):
        for s in range(2):
            for k in range(NY):
                n = (2 * w + s) * NY + k
                copies.append(
                    pltpu.make_async_copy(
                        arrays[k].at[pl.ds(s * rows, rows)],
                        cot_buf.at[2 * w + s, pl.ds(k * rows, rows)],
                        sems.at[n],
                    )
                )
                copies[-1].start()
    for j in range(NZ):
        place = ((y - z - j) & 3) * rows
        att_scr[:, pl.ds(pl.multiple_of(place, 128), rows)] = att_ref[j]
    for w in range(2):
        for s in range(2):
            for copy in copies[(2 * w + s) * NY : (2 * w + s + 1) * NY]:
                copy.wait()
            acc = dot_nn(att_scr[...], cot_buf[2 * w + s])
            target = (((zl ^ s) * 2 + (c ^ w)) - x) & 3

            for n in range(NX):

                @pl.when(target == n)
                def _(n=n, acc=acc):
                    outs[n][...] = acc.astype(outs[n].dtype)


def per_device(
    queries,
    local_keys,
    local_values,
    segments,
    memory_keys,
    memory_values,
    retrieved,
    block_slot,
    gate_bias,
    out_weight,
    cotangent,
):
    rows, width = queries.shape
    heads = width // HEAD
    mem, ten = lax.axis_index("mem"), lax.axis_index("tensor")
    z, x = mem // NX, mem % NX
    y, zl, c = ten // 4, (ten // 2) % 2, ten % 2
    ids = jnp.stack([z, x, y, jnp.zeros_like(z), zl, c]).astype(jnp.int32)
    gate = jax.nn.sigmoid(gate_bias)
    params = pltpu.CompilerParams(vmem_limit_bytes=16 << 20)

    names = jnp.arange(block_slot.shape[0], dtype=jnp.int32)
    storage = jnp.sum(
        jnp.where(retrieved.reshape(-1)[:, None] == names[None, :], block_slot[None, :], 0), axis=1
    )
    extra = jnp.zeros((EXTRA, width), jnp.bfloat16)
    extra = extra.at[0, 0 : storage.shape[0]].set(storage.astype(jnp.bfloat16))
    q_pack = jnp.concatenate([queries, extra], axis=0)

    k1, v3, q1, q3, moved, own_keys, own_values, own_cot, q_pack = together(
        shift_x(memory_keys, 1),
        shift_x(memory_values, -1),
        shift_z(q_pack, 1),
        shift_z(q_pack, 3),
        move_zy(cotangent, lambda z, y: (z, (y + z) % NY)),
        memory_keys,
        memory_values,
        cotangent,
        q_pack,
    )
    q2 = shift_z(q_pack, 2)
    swapped = move_zy(moved, lambda z, y: ((y - z) % NZ, y))
    v1, k2, v2 = shift_x(own_values, 1), shift_x(k1, 1), shift_x(v3, -1)
    k3 = shift_x(after(own_keys, v2), -1)
    early = stored_in(q_pack, q1, q3)
    q2, k2, v1, k3, swapped, own_cot, early = together(q2, k2, v1, k3, swapped, own_cot, early)
    near, near_own = flip_tensor(swapped, 2), flip_tensor(own_cot, 2)
    q_all = [q_pack, q1, q2, q3]

    local_out = pl.pallas_call(
        local_kernel,
        out_shape=jax.ShapeDtypeStruct((rows, width), jnp.float32),
        in_specs=[SM] + [VM] * 4,
        out_specs=VM,
        compiler_params=params,
        cost_estimate=cost(4 * heads * rows * rows * HEAD, heads * rows * rows, 6 * rows * width),
        name="local_attention",
    )(gate, segments.reshape(1, rows), queries, local_keys, local_values)

    parts = pl.pallas_call(
        memory_kernel,
        out_shape=jax.ShapeDtypeStruct((NZ, rows + EXTRA, width), jnp.bfloat16),
        in_specs=[SM] * 3 + [HB] * 12,
        out_specs=VM,
        scratch_shapes=[
            pltpu.VMEM((NZ, rows + EXTRA, width), jnp.bfloat16),
            pltpu.VMEM((NX, SLOTS * BLOCK, width), jnp.bfloat16),
            pltpu.VMEM((NX, SLOTS * BLOCK, width), jnp.bfloat16),
            pltpu.SMEM((2 * NZ * NX + 1,), jnp.int32),
            pltpu.SemaphoreType.DMA((12 * heads,)),
        ],
        compiler_params=params,
        cost_estimate=cost(
            64 * heads * rows * rows * HEAD, 8 * heads * rows * rows, 24 * rows * width
        ),
        name="memory_attention",
    )(ids, early, stored_in(q2), *in_hbm([*q_all, memory_keys, k1, k2, k3, memory_values, v1, v2, v3]))

    tall = jnp.concatenate([swapped, near], axis=0)
    wide = jnp.concatenate([cotangent, near_own], axis=0)
    parts, tall, wide = together(parts, tall, wide)
    back = exchange_z(parts)
    t1, t3, w1, w3 = [shift_y(v, k) for v in (tall, wide) for k in (1, 3)]
    back, t1, t3, w1, w3, tall, wide = together(back, t1, t3, w1, w3, tall, wide)
    t2 = shift_y(tall, 2)
    w2 = shift_y(after(wide, t2), 2)
    attention, att_t = pl.pallas_call(
        merge_kernel,
        out_shape=[
            jax.ShapeDtypeStruct((rows, width), jnp.bfloat16),
            jax.ShapeDtypeStruct((NZ, width, rows), jnp.bfloat16),
        ],
        in_specs=[SM] + [VM] * 2,
        out_specs=[VM] * 2,
        compiler_params=params,
        cost_estimate=cost(32 * rows * width, 4 * rows, 16 * rows * width),
        name="merge",
    )(gate, local_out, back)
    att_t, tall, wide, t1, t3, w1, w3 = together(att_t, tall, wide, t1, t3, w1, w3)
    att_all = exchange_z(att_t)
    tall, wide = [tall, t1, t2, t3], [wide, w1, w2, w3]
    flipped = [flip_tensor(v, 1) for v in tall + wide]
    att_all, *flipped = together(att_all, *flipped)
    tall, wide = in_hbm(tall + flipped[:4]), wide + flipped[4:]

    mine, *sent = pl.pallas_call(
        weight_kernel,
        out_shape=[jax.ShapeDtypeStruct((width, width), jnp.float32)]
        + [jax.ShapeDtypeStruct((width, width), jnp.bfloat16)] * 3,
        in_specs=[SM, VM] + [HB] * 8,
        out_specs=[VM] * 4,
        scratch_shapes=[
            pltpu.VMEM((width, NZ * rows), jnp.bfloat16),
            pltpu.VMEM((4, NY * rows, width), jnp.bfloat16),
            pltpu.SemaphoreType.DMA((16,)),
        ],
        compiler_params=params,
        cost_estimate=cost(32 * rows * width * width, 0, 48 * rows * width),
        name="weight_partials",
    )(ids, att_all, *tall)
    got = [shift_x(sent[n - 1], n) for n in (1, 3, 2)]
    attention_grad = pl.pallas_call(
        grad_kernel,
        out_shape=jax.ShapeDtypeStruct((rows, width), jnp.bfloat16),
        grid_spec=pltpu.PrefetchScalarGridSpec(
            num_scalar_prefetch=1,
            grid=(NY,),
            in_specs=[
                pl.BlockSpec(
                    (2 * rows, width), lambda g, ids: (0, 0), pipeline_mode=pl.Buffered(1)
                )
            ]
            * 8
            + [pl.BlockSpec((width, 4 * width), lambda g, ids: (0, (ids[2] - g) & 3))],
            out_specs=pl.BlockSpec((rows, width), lambda g, ids: (0, 0)),
            scratch_shapes=[pltpu.VMEM((rows, width), jnp.float32)],
        ),
        compiler_params=params,
        cost_estimate=cost(32 * rows * width * width, 0, 64 * rows * width),
        name="attention_grad",
    )(ids, *wide, *in_hbm([out_weight]))

    attention_grad, *got = together(attention_grad, *got)
    weight_grad = (mine + got[0].astype(jnp.float32)) + (
        got[1].astype(jnp.float32) + got[2].astype(jnp.float32)
    )
    return (attention, attention_grad, weight_grad)


def solution(mesh):
    return jax.shard_map(
        per_device,
        mesh=mesh,
        in_specs=(
            P("mem", "tensor"),
            P("mem", "tensor"),
            P("mem", "tensor"),
            P("mem"),
            P("mem", "tensor"),
            P("mem", "tensor"),
            P("mem", None),
            P(),
            P("tensor"),
            P("tensor", None),
            P("mem", "tensor"),
        ),
        out_specs=(P("mem", "tensor"), P("mem", "tensor"), P("tensor", "mem")),
        check_vma=False,
    )
```

```python
import jax
import jax.numpy as jnp
from jax import lax
from jax.experimental import pallas as pl
from jax.experimental.pallas import tpu as pltpu
from jax.sharding import PartitionSpec as P

HEAD = 128
BLOCK = 128
SLOTS = 4
NX = 4
NZ = 4
NY = 4
LOG2E = 1.4426950408889634
SCALE2 = HEAD**-0.5 * LOG2E
NEG = -1e30
EXTRA = 16

VM = pl.BlockSpec(memory_space=pltpu.VMEM)
SM = pl.BlockSpec(memory_space=pltpu.SMEM)
HB = pl.BlockSpec(memory_space=pltpu.HBM)


def cost(flops, transcendentals, bytes_accessed):
    return pl.CostEstimate(
        flops=flops, transcendentals=transcendentals, bytes_accessed=bytes_accessed
    )


def in_hbm(values):
    return [pltpu.with_memory_space_constraint(v, pltpu.HBM) for v in values]


def together(*values):
    return lax.optimization_barrier(values)


def after(value, *deps):
    return lax.optimization_barrier((value, *deps))[0]


def dot_nt(a, b):
    return lax.dot_general(a, b, (((1,), (1,)), ((), ())), preferred_element_type=jnp.float32)


def dot_nn(a, b):
    return lax.dot_general(a, b, (((1,), (0,)), ((), ())), preferred_element_type=jnp.float32)


def shift_x(value, k):
    pairs = [(z * NX + x, z * NX + (x + k) % NX) for z in range(NZ) for x in range(NX)]
    return lax.ppermute(value, "mem", pairs)


def shift_z(value, k):
    pairs = [(z * NX + x, (z + k) % NZ * NX + x) for z in range(NZ) for x in range(NX)]
    return lax.ppermute(value, "mem", pairs)


def exchange_z(value):
    groups = [[z * NX + x for z in range(NZ)] for x in range(NX)]
    return lax.all_to_all(
        value, "mem", split_axis=0, concat_axis=0, axis_index_groups=groups, tiled=True
    )


def shift_y(value, k):
    pairs = [(y * 4 + r, (y + k) % NY * 4 + r) for y in range(NY) for r in range(4)]
    return lax.ppermute(value, "tensor", pairs)


def gather_y(value):
    return [value] + [shift_y(value, k) for k in (1, 2, 3)]


def flip_tensor(value, bit):
    return lax.ppermute(value, "tensor", [(t, t ^ bit) for t in range(16)])


def stored_in(*packs):
    rows = packs[0].shape[0] - EXTRA
    return jnp.concatenate([q[rows, 0:16] for q in packs]).astype(jnp.int32)


def move_zy(value, target):
    pairs = []
    for z in range(NZ):
        for y in range(NY):
            to_z, to_y = target(z, y)
            for x in range(NX):
                for r in range(4):
                    source = (z * NX + x) * 16 + y * 4 + r
                    pairs.append((source, (to_z * NX + x) * 16 + to_y * 4 + r))
    return lax.ppermute(value, ("mem", "tensor"), pairs)


def local_kernel(gate_ref, seg_ref, q_ref, k_ref, v_ref, out_ref):
    rows = q_ref.shape[0]
    heads = q_ref.shape[1] // HEAD
    seg_cols = jnp.broadcast_to(seg_ref[...].astype(jnp.float32), (rows, rows))
    seg_rows = seg_cols.T
    row_ids = lax.broadcasted_iota(jnp.int32, (rows, rows), 0)
    col_ids = lax.broadcasted_iota(jnp.int32, (rows, rows), 1)
    allowed = (col_ids <= row_ids) & (seg_cols == seg_rows)
    for h in range(heads):
        cols = pl.ds(h * HEAD, HEAD)
        scores = jnp.where(allowed, dot_nt(q_ref[:, cols], k_ref[:, cols]) * SCALE2, NEG)
        top = jnp.max(scores, axis=1, keepdims=True)
        weights = jnp.exp2(scores - top)
        total = jnp.sum(weights, axis=1, keepdims=True)
        out = dot_nn(weights.astype(jnp.bfloat16), v_ref[:, cols])
        out_ref[:, cols] = out * ((1.0 - gate_ref[h]) / total)


def memory_kernel(ids_ref, early_ref, late_ref, *refs):
    sources, result_ref = refs[0:12], refs[12]
    q_buf, k_buf, v_buf, sel_ref, sems = refs[13:18]
    targets = [buf.at[n] for buf in (q_buf, k_buf, v_buf) for n in range(4)]
    heads = k_buf.shape[2] // HEAD
    copies = []
    for h in range(heads):
        cols = pl.ds(h * HEAD, HEAD)
        copies.append(
            [
                pltpu.make_async_copy(src.at[:, cols], dst.at[:, cols], sems.at[12 * h + n])
                for n, (src, dst) in enumerate(zip(sources, targets))
            ]
        )
        for copy in copies[h]:
            copy.start()

    z, x = ids_ref[0], ids_ref[1]
    for n in range(2 * NZ * NX):
        sel_ref[n] = -1
    for n in range(2 * NZ * 8):
        j = n // 16
        block = late_ref[n % 16] if j == 2 else early_ref[min(j, 2) * 16 + n % 16]
        shard = block // SLOTS
        place = n // 8 * NX + ((x - shard) & 3)
        sel_ref[jnp.where(shard // NX == z, place, 2 * NZ * NX)] = block % SLOTS

    sub = lax.broadcasted_iota(jnp.int32, (8, BLOCK), 0)
    stats = [jnp.zeros((8, BLOCK), jnp.float32) for _ in range(2 * NZ)]
    for h in range(heads):
        cols = pl.ds(h * HEAD, HEAD)
        for copy in copies[h]:
            copy.wait()
        for n in range(2 * NZ):
            j, b = n // 2, n % 2
            rows = pl.ds(b * BLOCK, BLOCK)
            slots = [sel_ref[n * NX + i] for i in range(NX)]
            places = [
                pl.ds(pl.multiple_of(jnp.maximum(slot, 0) * BLOCK, BLOCK), BLOCK) for slot in slots
            ]
            keys = jnp.concatenate([k_buf[i, places[i], cols] for i in range(NX)])
            values = jnp.concatenate([v_buf[i, places[i], cols] for i in range(NX)])
            products = dot_nt(keys, q_buf[j, rows, cols])
            scores = [
                products[i * BLOCK : (i + 1) * BLOCK] * SCALE2 + jnp.where(slots[i] >= 0, 0.0, NEG)
                for i in range(NX)
            ]
            peak = jnp.maximum(jnp.maximum(scores[0], scores[1]), jnp.maximum(scores[2], scores[3]))
            top = jnp.max(peak, axis=0, keepdims=True)
            weights = [jnp.exp2(s - top) for s in scores]
            total = jnp.sum(
                (weights[0] + weights[1]) + (weights[2] + weights[3]), axis=0, keepdims=True
            )
            inverse = 1.0 / total
            weights = jnp.concatenate([(w * inverse).astype(jnp.bfloat16) for w in weights])
            out = lax.dot_general(
                weights, values, (((0,), (0,)), ((), ())), preferred_element_type=jnp.float32
            )
            result_ref[(z - j) & 3, rows, cols] = out.astype(jnp.bfloat16)
            stats[n] = jnp.where(sub == h, top + jnp.log2(total), stats[n])
    for n in range(2 * NZ):
        stat = stats[n]
        high = stat.astype(jnp.bfloat16).astype(jnp.float32)
        mid = (stat - high).astype(jnp.bfloat16).astype(jnp.float32)
        low = (stat - high) - mid
        packed = jnp.concatenate(
            [high[0:4], mid[0:4], low[0:4], jnp.zeros((4, BLOCK), jnp.float32)], axis=0
        )
        target = result_ref.at[(z - n // 2) & 3]
        target[2 * BLOCK : 2 * BLOCK + EXTRA, pl.ds(n % 2 * BLOCK, BLOCK)] = packed.astype(
            jnp.bfloat16
        )
    for j in range(NZ):
        result_ref[j, 2 * BLOCK : 2 * BLOCK + EXTRA, 2 * BLOCK :] = jnp.zeros(
            (EXTRA, result_ref.shape[2] - 2 * BLOCK), jnp.bfloat16
        )


def merge_kernel(gate_ref, local_ref, back_ref, att_ref, att_t_ref):
    parts = [back_ref.at[n] for n in range(NZ)]
    heads = local_ref.shape[1] // HEAD
    for b in range(2):
        rows = pl.ds(b * BLOCK, BLOCK)
        logs = []
        for p in parts:
            s = p[2 * BLOCK : 2 * BLOCK + EXTRA, rows].astype(jnp.float32)
            logs.append((s[0:4] + s[4:8]) + s[8:12])
        top = jnp.maximum(jnp.maximum(logs[0], logs[1]), jnp.maximum(logs[2], logs[3]))
        shares = [jnp.exp2(s - top) for s in logs]
        total = (shares[0] + shares[1]) + (shares[2] + shares[3])
        shares = [s / total for s in shares]
        table = jnp.concatenate(shares + [jnp.zeros((BLOCK - 16, BLOCK), jnp.float32)], axis=0).T
        for h in range(heads):
            cols = pl.ds(h * HEAD, HEAD)
            acc = None
            for n, p in enumerate(parts):
                term = p[rows, cols].astype(jnp.float32) * table[:, 4 * n + h : 4 * n + h + 1]
                acc = term if acc is None else acc + term
            out = gate_ref[h] * acc + local_ref[rows, cols]
            att_ref[rows, cols] = out.astype(jnp.bfloat16)
            flipped = out.T.astype(jnp.bfloat16)
            for n in range(NZ):
                att_t_ref[n, cols, rows] = flipped


def grad_kernel(ids_ref, *refs):
    own, other, w_ref, out_ref, acc_ref = refs[0:4], refs[4:8], refs[8], refs[9], refs[10]
    step = pl.program_id(0)
    zl, c = ids_ref[4], ids_ref[5]
    width = own[0].shape[1]
    rows = out_ref.shape[0]

    @pl.when(step == 0)
    def _():
        acc_ref[...] = jnp.zeros_like(acc_ref)

    for k in range(NY):

        @pl.when(step == k)
        def _(k=k):
            acc = acc_ref[...]
            for w, arrays in enumerate((own, other)):
                for s in range(2):
                    place = (zl ^ s) * 2 + (c ^ w)
                    cols = pl.ds(pl.multiple_of(place * width, 128), width)
                    acc = acc + dot_nt(arrays[k][s * rows : (s + 1) * rows, :], w_ref[:, cols])
            acc_ref[...] = acc

    @pl.when(step == NY - 1)
    def _():
        out_ref[...] = acc_ref[...].astype(jnp.bfloat16)


def weight_kernel(ids_ref, *refs):
    att_ref, own, other = refs[0], refs[1:5], refs[5:9]
    outs, att_scr, cot_buf, sems = refs[9:13], refs[13], refs[14], refs[15]
    z, x, y, zl, c = ids_ref[0], ids_ref[1], ids_ref[2], ids_ref[4], ids_ref[5]
    rows = att_ref.shape[2]
    copies = []
    for w, arrays in enumerate((own, other)):
        for s in range(2):
            for k in range(NY):
                n = (2 * w + s) * NY + k
                copies.append(
                    pltpu.make_async_copy(
                        arrays[k].at[pl.ds(s * rows, rows)],
                        cot_buf.at[2 * w + s, pl.ds(k * rows, rows)],
                        sems.at[n],
                    )
                )
                copies[-1].start()
    for j in range(NZ):
        place = ((y - z - j) & 3) * rows
        att_scr[:, pl.ds(pl.multiple_of(place, 128), rows)] = att_ref[j]
    for w in range(2):
        for s in range(2):
            for copy in copies[(2 * w + s) * NY : (2 * w + s + 1) * NY]:
                copy.wait()
            acc = dot_nn(att_scr[...], cot_buf[2 * w + s])
            target = (((zl ^ s) * 2 + (c ^ w)) - x) & 3

            for n in range(NX):

                @pl.when(target == n)
                def _(n=n, acc=acc):
                    outs[n][...] = acc.astype(outs[n].dtype)


def per_device(
    queries,
    local_keys,
    local_values,
    segments,
    memory_keys,
    memory_values,
    retrieved,
    block_slot,
    gate_bias,
    out_weight,
    cotangent,
):
    rows, width = queries.shape
    heads = width // HEAD
    mem, ten = lax.axis_index("mem"), lax.axis_index("tensor")
    z, x = mem // NX, mem % NX
    y, zl, c = ten // 4, (ten // 2) % 2, ten % 2
    ids = jnp.stack([z, x, y, jnp.zeros_like(z), zl, c]).astype(jnp.int32)
    gate = jax.nn.sigmoid(gate_bias)
    params = pltpu.CompilerParams(vmem_limit_bytes=16 << 20)

    names = jnp.arange(block_slot.shape[0], dtype=jnp.int32)
    storage = jnp.sum(
        jnp.where(retrieved.reshape(-1)[:, None] == names[None, :], block_slot[None, :], 0), axis=1
    )
    extra = jnp.zeros((EXTRA, width), jnp.bfloat16)
    extra = extra.at[0, 0 : storage.shape[0]].set(storage.astype(jnp.bfloat16))
    q_pack = jnp.concatenate([queries, extra], axis=0)

    k1, v3, q1, q3, moved, own_keys, own_values, own_cot, q_pack = together(
        shift_x(memory_keys, 1),
        shift_x(memory_values, -1),
        shift_z(q_pack, 1),
        shift_z(q_pack, 3),
        move_zy(cotangent, lambda z, y: (z, (y + z) % NY)),
        memory_keys,
        memory_values,
        cotangent,
        q_pack,
    )
    q2 = shift_z(q_pack, 2)
    swapped = move_zy(moved, lambda z, y: ((y - z) % NZ, y))
    v1, k2, v2 = shift_x(own_values, 1), shift_x(k1, 1), shift_x(v3, -1)
    k3 = shift_x(after(own_keys, v2), -1)
    early = stored_in(q_pack, q1, q3)
    q2, k2, v1, k3, swapped, own_cot, early = together(q2, k2, v1, k3, swapped, own_cot, early)
    near, near_own = flip_tensor(swapped, 2), flip_tensor(own_cot, 2)
    q_all = [q_pack, q1, q2, q3]

    local_out = pl.pallas_call(
        local_kernel,
        out_shape=jax.ShapeDtypeStruct((rows, width), jnp.float32),
        in_specs=[SM] + [VM] * 4,
        out_specs=VM,
        compiler_params=params,
        cost_estimate=cost(4 * heads * rows * rows * HEAD, heads * rows * rows, 6 * rows * width),
        name="local_attention",
    )(gate, segments.reshape(1, rows), queries, local_keys, local_values)

    parts = pl.pallas_call(
        memory_kernel,
        out_shape=jax.ShapeDtypeStruct((NZ, rows + EXTRA, width), jnp.bfloat16),
        in_specs=[SM] * 3 + [HB] * 12,
        out_specs=VM,
        scratch_shapes=[
            pltpu.VMEM((NZ, rows + EXTRA, width), jnp.bfloat16),
            pltpu.VMEM((NX, SLOTS * BLOCK, width), jnp.bfloat16),
            pltpu.VMEM((NX, SLOTS * BLOCK, width), jnp.bfloat16),
            pltpu.SMEM((2 * NZ * NX + 1,), jnp.int32),
            pltpu.SemaphoreType.DMA((12 * heads,)),
        ],
        compiler_params=params,
        cost_estimate=cost(
            64 * heads * rows * rows * HEAD, 8 * heads * rows * rows, 24 * rows * width
        ),
        name="memory_attention",
    )(ids, early, stored_in(q2), *in_hbm([*q_all, memory_keys, k1, k2, k3, memory_values, v1, v2, v3]))

    parts, near, near_own = together(parts, near, near_own)
    tall = jnp.concatenate([swapped, near], axis=0)
    wide = jnp.concatenate([cotangent, near_own], axis=0)
    back = exchange_z(parts)
    t1, t3, w1, w3 = [shift_y(v, k) for v in (tall, wide) for k in (1, 3)]
    back, t1, t3, w1, w3, tall, wide = together(back, t1, t3, w1, w3, tall, wide)
    t2 = shift_y(tall, 2)
    w2 = shift_y(after(wide, t2), 2)
    attention, att_t = pl.pallas_call(
        merge_kernel,
        out_shape=[
            jax.ShapeDtypeStruct((rows, width), jnp.bfloat16),
            jax.ShapeDtypeStruct((NZ, width, rows), jnp.bfloat16),
        ],
        in_specs=[SM] + [VM] * 2,
        out_specs=[VM] * 2,
        compiler_params=params,
        cost_estimate=cost(32 * rows * width, 4 * rows, 16 * rows * width),
        name="merge",
    )(gate, local_out, back)
    att_t, tall, wide, t1, t3, w1, w3 = together(att_t, tall, wide, t1, t3, w1, w3)
    att_all = exchange_z(att_t)
    tall, wide = [tall, t1, t2, t3], [wide, w1, w2, w3]
    flipped = [flip_tensor(v, 1) for v in tall + wide]
    att_all, *flipped = together(att_all, *flipped)
    tall, wide = in_hbm(tall + flipped[:4]), wide + flipped[4:]

    mine, *sent = pl.pallas_call(
        weight_kernel,
        out_shape=[jax.ShapeDtypeStruct((width, width), jnp.float32)]
        + [jax.ShapeDtypeStruct((width, width), jnp.bfloat16)] * 3,
        in_specs=[SM, VM] + [HB] * 8,
        out_specs=[VM] * 4,
        scratch_shapes=[
            pltpu.VMEM((width, NZ * rows), jnp.bfloat16),
            pltpu.VMEM((4, NY * rows, width), jnp.bfloat16),
            pltpu.SemaphoreType.DMA((16,)),
        ],
        compiler_params=params,
        cost_estimate=cost(32 * rows * width * width, 0, 48 * rows * width),
        name="weight_partials",
    )(ids, att_all, *tall)
    got = [shift_x(sent[n - 1], n) for n in (2, 1, 3)]
    attention_grad = pl.pallas_call(
        grad_kernel,
        out_shape=jax.ShapeDtypeStruct((rows, width), jnp.bfloat16),
        grid_spec=pltpu.PrefetchScalarGridSpec(
            num_scalar_prefetch=1,
            grid=(NY,),
            in_specs=[
                pl.BlockSpec(
                    (2 * rows, width), lambda g, ids: (0, 0), pipeline_mode=pl.Buffered(1)
                )
            ]
            * 8
            + [pl.BlockSpec((width, 4 * width), lambda g, ids: (0, (ids[2] - g) & 3))],
            out_specs=pl.BlockSpec((rows, width), lambda g, ids: (0, 0)),
            scratch_shapes=[pltpu.VMEM((rows, width), jnp.float32)],
        ),
        compiler_params=params,
        cost_estimate=cost(32 * rows * width * width, 0, 64 * rows * width),
        name="attention_grad",
    )(ids, *wide, *in_hbm([out_weight]))

    attention_grad, *got = together(attention_grad, *got)
    weight_grad = (mine + got[0].astype(jnp.float32)) + (
        got[1].astype(jnp.float32) + got[2].astype(jnp.float32)
    )
    return (attention, attention_grad, weight_grad)


def solution(mesh):
    return jax.shard_map(
        per_device,
        mesh=mesh,
        in_specs=(
            P("mem", "tensor"),
            P("mem", "tensor"),
            P("mem", "tensor"),
            P("mem"),
            P("mem", "tensor"),
            P("mem", "tensor"),
            P("mem", None),
            P(),
            P("tensor"),
            P("tensor", None),
            P("mem", "tensor"),
        ),
        out_specs=(P("mem", "tensor"), P("mem", "tensor"), P("tensor", "mem")),
        check_vma=False,
    )
```
